32 devices in a mesh: px: 8 (over z, y), py: 4 (over x, core).
Axes of the slice: x: 2, y: 2, z: 4, core: 2. Of those that a mesh axis runs over, the one named last changes fastest.
Arguments:
- field: bfloat16 [2, 64, 64, 4096], P(None, 'px', 'py'), may hold values from -6 to 6
- cotangent: bfloat16 [2, 64, 64, 4096], P(None, 'px', 'py'), may hold values from -6 to 6
- taps: bfloat16 [3, 64, 64, 64], replicated, may hold values from -1 to 1.5, as said below
Outputs:
- mapped: bfloat16 [2, 64, 64, 4096], P(None, 'px', 'py')
- grad_field: bfloat16 [2, 64, 64, 4096], P(None, 'px', 'py')
- grad_taps: float32 [3, 64, 64, 64], P(None, 'px', 'py')
The draws below stay inside these ranges and needn't reach their ends.
Inputs may be any that keep to these rules, and one draw needn't show every extreme that they name: Every diagonal entry taps[a, 0, c, c] lies between 1 and 1.5, and every diagonal entry taps[a, t, c, c] with t >= 1 has magnitude at most 0.4 / 64.
All inputs are finite; a program needn't handle non-finite values.
Results may differ from the reference program's by a relative error of at most 0.018.
Values may be sent and summed in bfloat16 or wider, within the bound.
No kernel may reach another device: no remote copies, remote signals or barrier semaphores. Data moves between devices by JAX's collectives and lax.ppermute only.
A program may use at most 192 MiB of HBM per device.

```python
import math
import jax
import jax.numpy as jnp
from jax import lax

N = 64
C = 64
B = 2


def draw_taps(key, part):
    key_spread, key_leading, key_trailing = jax.random.split(key, 3)
    tap_shape = (3, N, C, C)
    spread_part = jax.random.truncated_normal(key_spread, -4.0, 4.0, tap_shape, jnp.float32) * (0.15 / math.sqrt(N))
    leading = jax.random.uniform(key_leading, (3, 1, C), jnp.float32, 1.0, 1.5)
    trailing = jax.random.uniform(key_trailing, (3, N, C), jnp.float32, -0.39 / N, 0.39 / N)
    anchor_row = (jnp.arange(N) == 0)[None, :, None]
    diag_vals = jnp.where(anchor_row, leading, trailing)
    eye_mat = jnp.eye(C, dtype=jnp.float32)
    return (spread_part * (1.0 - eye_mat) + diag_vals[..., None] * eye_mat).astype(jnp.bfloat16)


def level_of(own_key, extent, cuts, least, high):
    def one(axis_at, blocks):
        heights = jax.random.uniform(jax.random.fold_in(jax.random.fold_in(own_key, 6), axis_at), (blocks,), jnp.float32, least / len(cuts), high / len(cuts))
        return jnp.repeat(jnp.exp(heights), extent[axis_at] // blocks).reshape((-1,) + (1,) * (len(extent) - axis_at - 1))

    loudness = one(*cuts[0])
    for cut in cuts[1:]:
        loudness = loudness * one(*cut)
    return loudness


def scatter_about(rng, extent, scale, most, pieces=(), kind=jnp.bfloat16):
    gain = level_of(rng, extent, pieces, -0.22, 0.18) if pieces else 1.0
    drawn = jax.random.normal(rng, extent, jnp.float32) * scale * gain
    return jnp.minimum(jnp.maximum(drawn, -most), most).astype(kind)


def setup_inputs(seed: int = 0) -> dict:
    keys = jax.random.split(jax.random.key(seed), 4)
    field = scatter_about(keys[0], (B, N, N, N * C), 1.0, 6.0, ((1, 8), (2, 4)))
    cotangent = scatter_about(keys[1], (B, N, N, N * C), 1.0, 6.0, ((1, 8), (2, 4)))
    taps = draw_taps(jax.random.fold_in(keys[3], 71), 0)
    return dict(field=field, cotangent=cotangent, taps=taps)


def dft_tables(row_ids, col_ids, length):
    product = row_ids[:, None] * col_ids[None, :] % length
    angle = product.astype(jnp.float32) * (2.0 * math.pi / length)
    return (jnp.cos(angle), jnp.sin(angle))

def along(values, table, position):
    letters = 'abcdef'[:values.ndim]
    target = letters[:position] + 'k' + letters[position + 1:]
    return jnp.einsum(letters + ',k' + letters[position] + '->' + target, values.astype(jnp.float32), table.astype(jnp.float32))

def section(values, position, cos_b, sin_b, turn_sign, factor):
    direct = along(values, cos_b, position)
    crossed = along(values, sin_b, position)
    half = values.shape[-1] // 2
    turned = jnp.concatenate([crossed[..., half:], -crossed[..., :half]], -1)
    return ((direct + turn_sign * turned) * factor).astype(jnp.bfloat16)

def z_forward(values, cos_b, sin_b):
    direct = along(values, cos_b, 3)
    crossed = along(values, sin_b, 3)
    return jnp.concatenate([direct, -crossed], -1).astype(jnp.bfloat16)

def z_inverse(values, cos_b, sin_b, factor):
    half = values.shape[-1] // 2
    real_part = along(values[..., :half], cos_b, 3)
    imag_part = along(values[..., half:], sin_b, 3)
    return ((real_part - imag_part) * factor).astype(jnp.bfloat16)

def spectra(taps_axis, cos_b, sin_b):
    taps_f = taps_axis.astype(jnp.float32)
    real_w = jnp.einsum('kt,toi->koi', cos_b.astype(jnp.float32), taps_f)
    imag_w = -jnp.einsum('kt,toi->koi', sin_b.astype(jnp.float32), taps_f)
    upper = jnp.concatenate([real_w, -imag_w], 2)
    lower = jnp.concatenate([imag_w, real_w], 2)
    return jnp.concatenate([upper, lower], 1).astype(jnp.bfloat16)

def push(values, matrix, position):
    letters = 'abcde'
    return jnp.einsum(letters + ',' + letters[position] + 'fe->abcdf', values.astype(jnp.float32), matrix.astype(jnp.float32)).astype(jnp.bfloat16)

def pull(values, matrix, position):
    letters = 'abcde'
    return jnp.einsum(letters + ',' + letters[position] + 'ef->abcdf', values.astype(jnp.float32), matrix.astype(jnp.float32)).astype(jnp.bfloat16)

def outer(left, right, position):
    letters = 'abcde'
    return jnp.einsum('abcde,abcdf->' + letters[position] + 'ef', left.astype(jnp.float32), right.astype(jnp.float32))

def tap_terms(spectral, cos_f, sin_f, split_t, split_o):
    width = spectral.shape[1] // 2
    count = spectral.shape[0]
    real_g = spectral[:, :width, :width] + spectral[:, width:, width:]
    imag_g = spectral[:, :width, width:] - spectral[:, width:, :width]
    cos_r = cos_f.reshape(count, split_t, -1)
    sin_r = sin_f.reshape(count, split_t, -1)
    real_r = real_g.reshape(count, split_o, -1, width)
    imag_r = imag_g.reshape(count, split_o, -1, width)
    highest = lax.Precision.HIGHEST
    return jnp.einsum('kpu,kqvi->pquvi', cos_r, real_r, precision=highest) + jnp.einsum('kpu,kqvi->pquvi', sin_r, imag_r, precision=highest)

def log_terms(taps, row_ids, col_ids, length):
    highest = lax.Precision.HIGHEST
    diag_w = jnp.diagonal(taps.astype(jnp.float32), axis1=2, axis2=3)
    cos_full, sin_full = dft_tables(row_ids, row_ids, length)
    real_z = jnp.einsum('kt,atc->akc', cos_full, diag_w, precision=highest)
    imag_z = -jnp.einsum('kt,atc->akc', sin_full, diag_w, precision=highest)
    modulus = real_z * real_z + imag_z * imag_z
    cos_cols, sin_cols = dft_tables(row_ids, col_ids, length)
    summed = jnp.einsum('kt,akc->atc', cos_cols, real_z / modulus, precision=highest) - jnp.einsum('kt,akc->atc', sin_cols, imag_z / modulus, precision=highest)
    return summed / math.sqrt(length)

def reference(field, cotangent, taps):
    all_ids = jnp.arange(N, dtype=jnp.int32)
    cos_f, sin_f = dft_tables(all_ids, all_ids, N)
    cos_b = cos_f.astype(jnp.bfloat16)
    sin_b = sin_f.astype(jnp.bfloat16)

    def forward_three(values):
        spectral = z_forward(values.reshape(B, N, N, N, C), cos_b, sin_b)
        spectral = section(spectral, 2, cos_b, sin_b, 1.0, 1.0)
        return section(spectral, 1, cos_b, sin_b, 1.0, 1.0)

    def inverse_three(values):
        spatial = section(values, 1, cos_b, sin_b, -1.0, 1.0 / N)
        spatial = section(spatial, 2, cos_b, sin_b, -1.0, 1.0 / N)
        return z_inverse(spatial, cos_b, sin_b, 1.0 / N).reshape(B, N, N, N * C)
    field_hat = forward_three(field)
    cot_hat = forward_three(cotangent)
    lower_mask = jnp.tril(jnp.ones((C, C), jnp.float32))
    masked = (taps.astype(jnp.float32) * lower_mask).astype(jnp.bfloat16)
    mix_x = spectra(masked[0], cos_b, sin_b)
    mix_y = spectra(masked[1], cos_b, sin_b)
    mix_z = spectra(masked[2], cos_b, sin_b)
    first = push(field_hat, mix_z, 3)
    second = push(first, mix_y, 2)
    out_hat = push(second, mix_x, 1)
    back_two = pull(cot_hat, mix_x, 1)
    back_one = pull(back_two, mix_y, 2)
    back_hat = pull(back_one, mix_z, 3)
    grad_x_spec = outer(cot_hat, second, 1)
    grad_y_spec = outer(back_two, first, 2)
    grad_z_spec = outer(back_one, field_hat, 3)
    mapped = inverse_three(out_hat)
    grad_field = inverse_three(back_hat)
    data_scale = 1.0 / (float(N) ** 4 * math.sqrt(N))
    terms = jnp.stack([tap_terms(grad_x_spec, cos_f, sin_f, 1, 1).reshape(N, C, C), tap_terms(grad_y_spec, cos_f, sin_f, 1, 1).reshape(N, C, C), tap_terms(grad_z_spec, cos_f, sin_f, 1, 1).reshape(N, C, C)], 0) * data_scale
    log_part = log_terms(taps, all_ids, all_ids, N)
    eye_mat = jnp.eye(C, dtype=jnp.float32)
    grad_taps = lower_mask * (terms - log_part[:, :, None, :] * eye_mat)
    return (mapped, grad_field, grad_taps)
```

```python
import math

import jax
import jax.numpy as jnp
import numpy as np
from jax import lax
from jax.experimental import pallas as pl
from jax.experimental.pallas import tpu as pltpu
from jax.sharding import PartitionSpec as P

N = 64
C = 64
F32 = jnp.float32
BF16 = jnp.bfloat16


def real_dft(length):
    half = length // 2
    slot = np.arange(half)[:, None]
    at = np.arange(length)[None, :]
    angle = 2.0 * np.pi * ((slot * at) % length) / length
    real = np.cos(angle)
    imag = -np.sin(angle)
    imag[0] = (-1.0) ** np.arange(length)
    forward = np.concatenate([real, imag], 0)
    weight = np.where(np.arange(half) == 0, 1.0, 2.0) / length
    inverse = (forward * np.concatenate([weight, weight])[:, None]).T
    return forward, inverse


def line_table():
    at = np.arange(N)[None, :]
    freq = np.arange(N // 2 + 1)[:, None]
    angle = 2.0 * np.pi * ((freq * at) % N) / N
    return np.concatenate([np.cos(angle), -np.sin(angle[: N // 2]), np.zeros((7, N))], 0)


def pair_table():
    length = N // 2
    half = length // 2
    slot = np.arange(half)
    table = np.zeros((2, 2, 2, half, 2, N))
    for row in range(2):
        for col in range(2):
            for t in range((row + col) % 2, N, 2):
                lag = (t - col + row) // 2
                angle = 2.0 * np.pi * ((slot * lag) % length) / length
                cos, sin = np.cos(angle), np.sin(angle)
                other = cos.copy()
                other[0] = (-1.0) ** lag
                sin[0] = 0.0
                table[col, 0, 0, :, row, t] = cos
                table[col, 1, 1, :, row, t] = other
                table[col, 0, 1, :, row, t] = -sin
                table[col, 1, 0, :, row, t] = sin
    return table.reshape(8 * half, 2 * N)


def lag_rows(length, lag):
    half = length // 2
    slot = np.arange(half)
    angle = 2.0 * np.pi * ((slot * lag) % length) / length
    weight = np.where(slot == 0, 1.0, 2.0) / length
    real = np.cos(angle) * weight
    imag = np.sin(angle) * weight
    imag[0] = (-1.0) ** lag / length
    return np.concatenate([real, imag])


def tap_tables():
    scale = float(N) ** -1.5
    half = N // 2
    direct = np.stack([lag_rows(N, t) for t in range(N)], 0)
    paired = np.stack([np.concatenate([lag_rows(half, d), lag_rows(half, d + 1)]) for d in range(half)], 0)
    return direct * scale, paired * scale


def dot(a, b):
    return jnp.dot(a, b, preferred_element_type=F32)


def dot_nt(a, b):
    return lax.dot_general(a, b, (((1,), (1,)), ((), ())), preferred_element_type=F32)


def dot_tn(a, b):
    return lax.dot_general(a, b, (((0,), (0,)), ((), ())), preferred_element_type=F32)


def whole(count):
    return [pl.BlockSpec(memory_space=pltpu.VMEM)] * count


def params(megabytes):
    return pltpu.CompilerParams(vmem_limit_bytes=megabytes << 20)


def expand_to(out_ref, table_ref, row_of, col_of, row_lane, col_lane):
    size = out_ref.shape[0]
    small_rows, small_cols = table_ref.shape
    pick = lax.broadcasted_iota(jnp.int32, (small_cols, size), 0)
    wide = lax.broadcasted_iota(jnp.int32, (small_cols, size), 1)
    columns = jnp.where(pick == col_of(wide), 1.0, 0.0).astype(BF16)
    chunk = 256

    @pl.loop(0, size // chunk)
    def _(step):
        base = step * chunk
        tall = lax.broadcasted_iota(jnp.int32, (chunk, small_rows), 0) + base
        which = lax.broadcasted_iota(jnp.int32, (chunk, small_rows), 1)
        rows = jnp.where(row_of(tall) == which, 1.0, 0.0).astype(BF16)
        values = dot(dot(rows, table_ref[...]).astype(BF16), columns)
        at_row = lax.broadcasted_iota(jnp.int32, (chunk, size), 0) + base
        at_col = lax.broadcasted_iota(jnp.int32, (chunk, size), 1)
        keep = row_lane(at_row) == col_lane(at_col)
        out_ref[pl.ds(pl.multiple_of(base, chunk), chunk), :] = jnp.where(keep, values, 0.0).astype(BF16)


def high(v):
    return v // 16


def low(v):
    return v % 16


def y_position(v):
    return (v // 256) * 16 + v % 16


def y_lane(v):
    return (v // 16) % 16


def tables_kernel(fwd, inv, fwd_z, inv_z, fx, ix, fy, iy, fz, iz):
    expand_to(fz, fwd_z, high, high, low, low)
    expand_to(iz, inv_z, high, high, low, low)
    expand_to(fx, fwd, high, high, low, low)
    expand_to(ix, inv, high, high, low, low)
    expand_to(fy, fwd, high, y_position, low, y_lane)
    expand_to(iy, inv, y_position, high, y_lane, low)


def tables(fwd, inv, fwd_z, inv_z):
    big = jax.ShapeDtypeStruct((1024, 1024), BF16)
    small = jax.ShapeDtypeStruct((512, 512), BF16)
    return pl.pallas_call(
        tables_kernel,
        out_shape=(big, big, big, big, small, small),
        in_specs=whole(4),
        out_specs=tuple(whole(6)),
        compiler_params=params(40),
        cost_estimate=pl.CostEstimate(flops=2 << 30, bytes_accessed=12 << 20, transcendentals=0),
        name="tables",
    )(fwd, inv, fwd_z, inv_z)


def mixing_kernel(taps, e_line, e_pair, mix_x, mix_y, mix_z, wide, lines, pairs):
    row = lax.broadcasted_iota(jnp.int32, (64, 64, 64), 1)
    col = lax.broadcasted_iota(jnp.int32, (64, 64, 64), 2)
    for axis in range(3):
        masked = jnp.where(col <= row, taps[axis].astype(F32), 0.0).reshape(4096, 64)
        wide[:, :64] = masked
        wide[:, 64:] = jnp.zeros_like(masked)

        if axis < 2:
            out = mix_x if axis == 0 else mix_y

            @pl.loop(0, 64, unroll=8)
            def _(co):
                at = wide[pl.ds(co, 64, stride=64), :].astype(BF16)
                lines[pl.ds(co, 72, stride=64), :] = dot(e_line[...], at)

            @pl.loop(0, 32, unroll=4)
            def _(slot):
                def block(index):
                    one = lines[pl.ds(pl.multiple_of(index * 64, 64), 64), :]
                    return jnp.concatenate([one, pltpu.roll(one, 64, 1)], 0)

                imag = block(33 + slot)
                out[0, 0, slot] = block(slot).astype(BF16)
                out[1, 1, slot] = block(jnp.where(slot == 0, 32, slot)).astype(BF16)
                out[1, 0, slot] = imag.astype(BF16)
                out[0, 1, slot] = (-imag).astype(BF16)

        else:

            @pl.loop(0, 64, unroll=8)
            def _(co):
                at = wide[pl.ds(co, 64, stride=64), :]
                both = jnp.concatenate([at, pltpu.roll(at, 64, 1)], 0).astype(BF16)
                got = dot(e_pair[...], both)
                pairs[pl.ds(co, 64, stride=128), :] = got[:64]
                pairs[pl.ds(co + 64, 64, stride=128), :] = got[64:]

            for ri in range(2):
                for to in range(2):

                    @pl.loop(0, 16, unroll=4)
                    def _(slot):
                        start = ((ri * 2 + to) * 16 + slot) * 128
                        mix_z[to, ri, slot] = pairs[pl.ds(pl.multiple_of(start, 128), 128), :].astype(BF16)


def mixing(taps, e_line, e_pair):
    line = jax.ShapeDtypeStruct((2, 2, 32, 128, 128), BF16)
    pair = jax.ShapeDtypeStruct((2, 2, 16, 128, 128), BF16)
    return pl.pallas_call(
        mixing_kernel,
        out_shape=(line, line, pair),
        in_specs=whole(3),
        out_specs=tuple(whole(3)),
        scratch_shapes=[
            pltpu.VMEM((4096, 128), F32),
            pltpu.VMEM((72 * 64, 128), F32),
            pltpu.VMEM((64 * 128, 128), F32),
        ],
        compiler_params=params(40),
        cost_estimate=pl.CostEstimate(flops=2 << 30, bytes_accessed=12 << 20, transcendentals=0),
        name="mixing",
    )(taps, e_line, e_pair)


def mix_matrix(mix_ref, slot):
    top = jnp.concatenate([mix_ref[0, 0, slot], mix_ref[0, 1, slot]], 1)
    bottom = jnp.concatenate([mix_ref[1, 0, slot], mix_ref[1, 1, slot]], 1)
    return jnp.concatenate([top, bottom], 0)


def mix_apply(val, matrix, adjoint):
    return (dot(val, matrix) if adjoint else dot_nt(val, matrix)).astype(BF16)


def gradient_blocks(cot, val, slot):
    outer = dot_tn(cot, val)
    first = slot == 0
    real_real = outer[:128, :128]
    imag_imag = outer[128:, 128:]
    crossed = outer[:128, 128:] - outer[128:, :128]
    real = jnp.where(first, real_real, real_real + imag_imag)
    imag = jnp.where(first, imag_imag, crossed)
    return real, imag


def to_lags(table, sums, out):
    lags, depth = table.shape

    @pl.loop(0, 64, unroll=8)
    def _(co):
        rows = sums[pl.ds(co, depth, stride=64), :]
        out[pl.ds(co, lags, stride=64), :] = jnp.dot(
            table[...], rows, preferred_element_type=F32, precision=lax.Precision.HIGHEST
        )


def line_pass(axis, adjoint, values, fwd, inv, mix, out, spec, mixed, rhs, accumulate=None):
    @pl.loop(0, 4)
    def _(j):
        for h in range(2):
            block = values[:, j, h] if axis == "x" else values[2 * j + h]
            rhs[:, h * 128 : (h + 1) * 128] = block.reshape(1024, 128)
        for ri in range(2):
            for part in range(2):
                start = ri * 512 + part * 256
                got = dot(fwd[start : start + 256, :], rhs[...]).astype(BF16).reshape(16, 16, 256)
                for h in range(2):
                    spec[part * 16 : (part + 1) * 16, 2 * j + h, :, ri * 128 : (ri + 1) * 128] = got[
                        :, :, h * 128 : (h + 1) * 128
                    ]

    @pl.loop(0, 32, unroll=4)
    def _(slot):
        val = spec[slot].reshape(128, 256)
        mixed[slot] = mix_apply(val, mix_matrix(mix, slot), adjoint).reshape(8, 16, 256)
        if accumulate is not None:
            accumulate(slot, val)

    @pl.loop(0, 4)
    def _(j):
        for h in range(2):
            for ri in range(2):
                rhs[ri * 512 : (ri + 1) * 512, h * 128 : (h + 1) * 128] = mixed[
                    :, 2 * j + h, :, ri * 128 : (ri + 1) * 128
                ].reshape(512, 128)
        for part in range(4):
            got = dot(inv[part * 256 : (part + 1) * 256, :], rhs[...]).astype(BF16)
            for h in range(2):
                piece = got[:, h * 128 : (h + 1) * 128].reshape(2, 8, 16, 128)
                if axis == "x":
                    out[part * 2 : (part + 1) * 2, j, h] = piece
                else:
                    out[2 * j + h, part] = piece


def planes_adjoint_kernel(values, fx, ix, fy, iy, mix_x, mix_y, out, spec_x, spec_y, between, mixed, rhs):
    line_pass("x", True, values, fx, ix, mix_x, between, spec_x, mixed, rhs)
    line_pass("y", True, between, fy, iy, mix_y, out, spec_y, mixed, rhs)


def planes_kernel(
    values, fx, ix, fy, iy, mix_x, mix_y, cot_x, cot_y, table, out, terms, between, spec, mixed, rhs, sums
):
    lane = lax.broadcasted_iota(jnp.int32, (64, 128), 1)

    def add_y(slot, val):
        blocks = gradient_blocks(cot_y[slot].reshape(128, 256), val, slot)
        for ri in range(2):
            at = pl.ds(pl.multiple_of((ri * 32 + slot) * 64, 64), 64)
            sums[at, :] = blocks[ri][64:] + pltpu.roll(blocks[ri][:64], 64, 1)

    def add_x(slot, val):
        blocks = gradient_blocks(cot_x[slot].reshape(128, 256), val, slot)
        for ri in range(2):
            at = pl.ds(pl.multiple_of((ri * 32 + slot) * 64, 64), 64)
            got = blocks[ri][:64] + pltpu.roll(blocks[ri][64:], 64, 1)
            sums[at, :] = jnp.where(lane < 64, got, sums[at, :])

    line_pass("y", False, values, fy, iy, mix_y, between, spec, mixed, rhs, add_y)
    line_pass("x", False, between, fx, ix, mix_x, out, spec, mixed, rhs, add_x)
    to_lags(table, sums, terms)


SPEC = (32, 8, 16, 256)


def planes_adjoint(values, fx, ix, fy, iy, mix_x, mix_y):
    spec = jax.ShapeDtypeStruct(SPEC, BF16)
    return pl.pallas_call(
        planes_adjoint_kernel,
        out_shape=(jax.ShapeDtypeStruct(values.shape, BF16), spec, spec),
        in_specs=whole(7),
        out_specs=tuple(whole(3)),
        scratch_shapes=[
            pltpu.VMEM(values.shape, BF16),
            pltpu.VMEM(SPEC, BF16),
            pltpu.VMEM((1024, 256), BF16),
        ],
        compiler_params=params(44),
        cost_estimate=pl.CostEstimate(flops=10 << 30, bytes_accessed=24 << 20, transcendentals=0),
        name="planes_adjoint",
    )(values, fx, ix, fy, iy, mix_x, mix_y)


def planes(values, fx, ix, fy, iy, mix_x, mix_y, cot_x, cot_y, table):
    return pl.pallas_call(
        planes_kernel,
        out_shape=(
            jax.ShapeDtypeStruct(values.shape, BF16),
            jax.ShapeDtypeStruct((4096, 128), F32),
        ),
        in_specs=whole(10),
        out_specs=tuple(whole(2)),
        scratch_shapes=[
            pltpu.VMEM(values.shape, BF16),
            pltpu.VMEM(SPEC, BF16),
            pltpu.VMEM(SPEC, BF16),
            pltpu.VMEM((1024, 256), BF16),
            pltpu.VMEM((4096, 128), F32),
        ],
        compiler_params=params(44),
        cost_estimate=pl.CostEstimate(flops=12 << 30, bytes_accessed=28 << 20, transcendentals=0),
        name="planes",
    )(values, fx, ix, fy, iy, mix_x, mix_y, cot_x, cot_y, table)


def depth_pass(adjoint, values, fwd, inv, mix, out, spec, mixed, rhs, accumulate=None):
    @pl.loop(0, 8)
    def _(j):
        for h in range(2):
            lanes = slice(h * 128, (h + 1) * 128)
            if adjoint:
                rhs[:, lanes] = values[:, 2 * j + h].reshape(512, 128)
            else:
                for zp in range(32):
                    rhs[zp * 16 : (zp + 1) * 16, lanes] = values[2 * j + h, :, zp * 128 : (zp + 1) * 128]
        for ri in range(2):
            got = dot(fwd[ri * 256 : (ri + 1) * 256, :], rhs[...]).astype(BF16).reshape(16, 16, 256)
            for h in range(2):
                spec[:, 2 * j + h, :, ri * 128 : (ri + 1) * 128] = got[:, :, h * 128 : (h + 1) * 128]

    @pl.loop(0, 16, unroll=4)
    def _(slot):
        val = spec[slot].reshape(256, 256)
        mixed[slot] = mix_apply(val, mix_matrix(mix, slot), adjoint).reshape(16, 16, 256)
        if accumulate is not None:
            accumulate(slot, val)

    @pl.loop(0, 8)
    def _(j):
        for h in range(2):
            for ri in range(2):
                rhs[ri * 256 : (ri + 1) * 256, h * 128 : (h + 1) * 128] = mixed[
                    :, 2 * j + h, :, ri * 128 : (ri + 1) * 128
                ].reshape(256, 128)
        for part in range(2):
            got = dot(inv[part * 256 : (part + 1) * 256, :], rhs[...]).astype(BF16)
            for h in range(2):
                lanes = slice(h * 128, (h + 1) * 128)
                if adjoint:
                    for zp in range(16):
                        place = (part * 16 + zp) * 128
                        out[2 * j + h, :, place : place + 128] = got[zp * 16 : (zp + 1) * 16, lanes]
                else:
                    out[part * 16 : (part + 1) * 16, 2 * j + h] = got[:, lanes].reshape(16, 16, 128)


DEPTH_SPEC = (16, 16, 16, 256)


def depth_kernel(values, fwd, inv, mix, out, spec, mixed, rhs):
    depth_pass(False, values, fwd, inv, mix, out, spec, mixed, rhs)


def depth_adjoint_kernel(values, fwd, inv, mix, other, table, out, terms, spec, mixed, rhs, sums):
    lane = lax.broadcasted_iota(jnp.int32, (64, 128), 1)

    def add_z(slot, val):
        blocks = gradient_blocks(val, other[slot].reshape(256, 256), slot)
        for ri in range(2):
            top, bottom = blocks[ri][:64], pltpu.roll(blocks[ri][64:], 64, 1)
            at = pl.multiple_of((ri * 16 + slot) * 64, 64)
            sums[pl.ds(at, 64), :] = jnp.where(lane < 64, top, 0.0) + bottom
            sums[pl.ds(at + 2048, 64), :] = jnp.where(lane < 64, 0.0, top)

    depth_pass(True, values, fwd, inv, mix, out, spec, mixed, rhs, add_z)
    to_lags(table, sums, terms)


def depth(values, fwd, inv, mix):
    return pl.pallas_call(
        depth_kernel,
        out_shape=(
            jax.ShapeDtypeStruct((32, 16, 16, 128), BF16),
            jax.ShapeDtypeStruct(DEPTH_SPEC, BF16),
        ),
        in_specs=whole(4),
        out_specs=tuple(whole(2)),
        scratch_shapes=[pltpu.VMEM(DEPTH_SPEC, BF16), pltpu.VMEM((512, 256), BF16)],
        compiler_params=params(24),
        cost_estimate=pl.CostEstimate(flops=4 << 30, bytes_accessed=10 << 20, transcendentals=0),
        name="depth",
    )(values, fwd, inv, mix)


def depth_adjoint(values, fwd, inv, mix, other, table):
    return pl.pallas_call(
        depth_adjoint_kernel,
        out_shape=(
            jax.ShapeDtypeStruct((16, 16, 4096), BF16),
            jax.ShapeDtypeStruct((2048, 128), F32),
        ),
        in_specs=whole(6),
        out_specs=tuple(whole(2)),
        scratch_shapes=[
            pltpu.VMEM(DEPTH_SPEC, BF16),
            pltpu.VMEM(DEPTH_SPEC, BF16),
            pltpu.VMEM((512, 256), BF16),
            pltpu.VMEM((4096, 128), F32),
        ],
        compiler_params=params(32),
        cost_estimate=pl.CostEstimate(flops=6 << 30, bytes_accessed=12 << 20, transcendentals=0),
        name="depth_adjoint",
    )(values, fwd, inv, mix, other, table)


def dft_tables(row_ids, col_ids, length):
    product = row_ids[:, None] * col_ids[None, :] % length
    angle = product.astype(jnp.float32) * (2.0 * math.pi / length)
    return (jnp.cos(angle), jnp.sin(angle))


def log_terms(taps, row_ids, col_ids, length):
    highest = lax.Precision.HIGHEST
    diag_w = jnp.diagonal(taps.astype(jnp.float32), axis1=2, axis2=3)
    cos_full, sin_full = dft_tables(row_ids, row_ids, length)
    real_z = jnp.einsum("kt,atc->akc", cos_full, diag_w, precision=highest)
    imag_z = -jnp.einsum("kt,atc->akc", sin_full, diag_w, precision=highest)
    modulus = real_z * real_z + imag_z * imag_z
    cos_cols, sin_cols = dft_tables(row_ids, col_ids, length)
    summed = jnp.einsum("kt,akc->atc", cos_cols, real_z / modulus, precision=highest) - jnp.einsum(
        "kt,akc->atc", sin_cols, imag_z / modulus, precision=highest
    )
    return summed / math.sqrt(length)


def own_log_terms(taps, count_px):
    all_ids = jnp.arange(N, dtype=jnp.int32)
    slab_t = N // count_px
    t_ids = lax.axis_index("px") * slab_t + jnp.arange(slab_t, dtype=jnp.int32)
    return log_terms(taps, all_ids, t_ids, N)


def finish_taps(summed, log_part, count_py):
    slab_o = C // count_py
    o_ids = lax.axis_index("py") * slab_o + jnp.arange(slab_o, dtype=jnp.int32)
    channel_ids = jnp.arange(C, dtype=jnp.int32)
    diagonal_sel = (channel_ids[None, :] == o_ids[:, None]).astype(jnp.float32)
    keep_mask = (channel_ids[None, :] <= o_ids[:, None]).astype(jnp.float32)
    return keep_mask * (summed - log_part[:, :, None, :] * diagonal_sel)


def halve(values, dim, axis, bit):
    count = lax.axis_size(axis)
    mine = (lax.axis_index(axis) >> bit) & 1
    keep = lax.dynamic_index_in_dim(values, mine, dim, keepdims=False)
    send = lax.dynamic_index_in_dim(values, 1 - mine, dim, keepdims=False).astype(BF16)
    got = lax.ppermute(send, axis, [(i, i ^ (1 << bit)) for i in range(count)])
    return keep + got.astype(F32)


def plane_device(field, cotangent, taps):
    axes = ("px", "py")
    count_px = lax.axis_size("px")
    count_py = lax.axis_size("py")
    shape = field.shape
    count = count_px * count_py
    column_shape = (count, 16, 16, 128)
    plane_shape = (count_px, count_py, 2, 8, 16, 128)

    def exchange(values):
        return lax.all_to_all(values, axes, 0, 0, tiled=True)

    cot_pairs = cotangent.reshape(16, 16, count, 128).transpose(2, 0, 1, 3)
    cot_planes = exchange(cot_pairs).reshape(plane_shape)

    small = real_dft(N) + real_dft(N // 2)
    fx, ix, fy, iy, fz, iz = tables(*[jnp.asarray(v, BF16) for v in small])
    mix_x, mix_y, mix_z = mixing(taps, jnp.asarray(line_table(), BF16), jnp.asarray(pair_table(), BF16))
    direct, paired = [jnp.asarray(v, F32) for v in tap_tables()]

    first, field_spec = depth(field.reshape(16, 16, 4096), fz, iz, mix_z)
    first_planes = exchange(first).reshape(plane_shape)

    fx_then, log_part = lax.optimization_barrier((fx, own_log_terms(taps, count_px)))
    back_one, cot_spec, back_spec = planes_adjoint(cot_planes, fx_then, ix, fy, iy, mix_x, mix_y)
    back_columns = exchange(back_one.reshape(column_shape))

    out, terms_xy = planes(first_planes, fx, ix, fy, iy, mix_x, mix_y, cot_spec, back_spec, direct)
    out_columns = exchange(out.reshape(column_shape))

    grad_field, terms_z = depth_adjoint(back_columns, fz, iz, mix_z, field_spec, paired)
    mapped = out_columns.transpose(1, 2, 0, 3).reshape(shape)

    terms = jnp.concatenate([terms_xy.reshape(8, 8, N, 128), terms_z.reshape(8, 4, N, 128)], 1)
    terms = terms.reshape(2, 2, 2, 12, 2, 2, 16, 128)
    for dim, axis, bit in ((5, "py", 0), (4, "py", 1), (2, "px", 0), (1, "px", 1), (0, "px", 2)):
        terms = halve(terms, dim, axis, bit)
    along_z = terms[8:].reshape(4, 16, 2, C).transpose(0, 2, 1, 3).reshape(8, 16, C)
    summed = jnp.stack([terms[:8, :, :C], terms[:8, :, C:], along_z], 0)
    grad_taps = finish_taps(summed, log_part, count_py)
    return (mapped, grad_field.reshape(shape), grad_taps)


def along(values, table, position):
    letters = "abcdef"[: values.ndim]
    target = letters[:position] + "k" + letters[position + 1 :]
    return jnp.einsum(
        letters + ",k" + letters[position] + "->" + target,
        values,
        table,
        preferred_element_type=jnp.float32,
    )


def section(values, position, cos_b, sin_b, turn_sign, factor):
    direct = along(values, cos_b, position)
    crossed = along(values, sin_b, position)
    half = values.shape[-1] // 2
    turned = jnp.concatenate([crossed[..., half:], -crossed[..., :half]], -1)
    return ((direct + turn_sign * turned) * factor).astype(jnp.bfloat16)


def z_forward(values, cos_b, sin_b):
    direct = along(values, cos_b, 3)
    crossed = along(values, sin_b, 3)
    return jnp.concatenate([direct, -crossed], -1).astype(jnp.bfloat16)


def z_inverse(values, cos_b, sin_b, factor):
    half = values.shape[-1] // 2
    real_part = along(values[..., :half], cos_b, 3)
    imag_part = along(values[..., half:], sin_b, 3)
    return ((real_part - imag_part) * factor).astype(jnp.bfloat16)


def spectra(taps_axis, cos_b, sin_b):
    real_w = jnp.einsum("kt,toi->koi", cos_b, taps_axis, preferred_element_type=jnp.float32)
    imag_w = -jnp.einsum("kt,toi->koi", sin_b, taps_axis, preferred_element_type=jnp.float32)
    upper = jnp.concatenate([real_w, -imag_w], 2)
    lower = jnp.concatenate([imag_w, real_w], 2)
    return jnp.concatenate([upper, lower], 1).astype(jnp.bfloat16)


def push(values, matrix, position):
    letters = "abcde"
    return jnp.einsum(
        letters + "," + letters[position] + "fe->abcdf",
        values,
        matrix,
        preferred_element_type=jnp.float32,
    ).astype(jnp.bfloat16)


def pull(values, matrix, position):
    letters = "abcde"
    return jnp.einsum(
        letters + "," + letters[position] + "ef->abcdf",
        values,
        matrix,
        preferred_element_type=jnp.float32,
    ).astype(jnp.bfloat16)


def outer(left, right, position):
    letters = "abcde"
    return jnp.einsum(
        "abcde,abcdf->" + letters[position] + "ef", left, right, preferred_element_type=jnp.float32
    )


def tap_terms(spectral, cos_f, sin_f, split_t, split_o):
    width = spectral.shape[1] // 2
    count = spectral.shape[0]
    real_g = spectral[:, :width, :width] + spectral[:, width:, width:]
    imag_g = spectral[:, :width, width:] - spectral[:, width:, :width]
    cos_r = cos_f.reshape(count, split_t, -1)
    sin_r = sin_f.reshape(count, split_t, -1)
    real_r = real_g.reshape(count, split_o, -1, width)
    imag_r = imag_g.reshape(count, split_o, -1, width)
    highest = lax.Precision.HIGHEST
    return jnp.einsum("kpu,kqvi->pquvi", cos_r, real_r, precision=highest) + jnp.einsum(
        "kpu,kqvi->pquvi", sin_r, imag_r, precision=highest
    )


def line_device(field, cotangent, taps):
    batch_rows = field.shape[0]
    local_x = field.shape[1]
    local_y = field.shape[2]
    count_px = lax.axis_size("px")
    count_py = lax.axis_size("py")
    all_ids = jnp.arange(N, dtype=jnp.int32)
    cos_f, sin_f = dft_tables(all_ids, all_ids, N)
    cos_b = cos_f.astype(jnp.bfloat16)
    sin_b = sin_f.astype(jnp.bfloat16)
    stacked = jnp.concatenate([field, cotangent], 0).reshape(2 * batch_rows, local_x, local_y, N, C)
    spectral = z_forward(stacked, cos_b, sin_b)
    spectral = section(
        lax.all_to_all(spectral, "py", split_axis=3, concat_axis=2, tiled=True),
        2,
        cos_b,
        sin_b,
        1.0,
        1.0,
    )
    spectral = section(
        lax.all_to_all(spectral, "px", split_axis=2, concat_axis=1, tiled=True),
        1,
        cos_b,
        sin_b,
        1.0,
        1.0,
    )
    field_hat = spectral[:batch_rows]
    cot_hat = spectral[batch_rows:]
    count_ky = N // count_px
    count_kz = N // count_py
    ky_ids = lax.axis_index("px") * count_ky + jnp.arange(count_ky, dtype=jnp.int32)
    kz_ids = lax.axis_index("py") * count_kz + jnp.arange(count_kz, dtype=jnp.int32)
    cos_y, sin_y = dft_tables(ky_ids, all_ids, N)
    cos_z, sin_z = dft_tables(kz_ids, all_ids, N)
    lower_mask = jnp.tril(jnp.ones((C, C), jnp.float32))
    masked = (taps.astype(jnp.float32) * lower_mask).astype(jnp.bfloat16)
    mix_x = spectra(masked[0], cos_b, sin_b)
    mix_y = spectra(masked[1], cos_y.astype(jnp.bfloat16), sin_y.astype(jnp.bfloat16))
    mix_z = spectra(masked[2], cos_z.astype(jnp.bfloat16), sin_z.astype(jnp.bfloat16))
    first = push(field_hat, mix_z, 3)
    second = push(first, mix_y, 2)
    out_hat = push(second, mix_x, 1)
    back_two = pull(cot_hat, mix_x, 1)
    back_one = pull(back_two, mix_y, 2)
    back_hat = pull(back_one, mix_z, 3)
    grad_x_spec = outer(cot_hat, second, 1)
    grad_y_spec = outer(back_two, first, 2)
    grad_z_spec = outer(back_one, field_hat, 3)
    returned = section(jnp.concatenate([out_hat, back_hat], 0), 1, cos_b, sin_b, -1.0, 1.0 / N)
    returned = section(
        lax.all_to_all(returned, "px", split_axis=1, concat_axis=2, tiled=True),
        2,
        cos_b,
        sin_b,
        -1.0,
        1.0 / N,
    )
    returned = z_inverse(
        lax.all_to_all(returned, "py", split_axis=2, concat_axis=3, tiled=True),
        cos_b,
        sin_b,
        1.0 / N,
    )
    returned = returned.reshape(2 * batch_rows, local_x, local_y, N * C)
    mapped = returned[:batch_rows]
    grad_field = returned[batch_rows:]
    data_scale = 1.0 / (float(N) ** 4 * math.sqrt(N))
    terms = (
        jnp.stack(
            [
                tap_terms(grad_x_spec, cos_f, sin_f, 1, 1),
                tap_terms(grad_y_spec, cos_y, sin_y, 1, 1),
                tap_terms(grad_z_spec, cos_z, sin_z, 1, 1),
            ],
            2,
        )
        * data_scale
    ).reshape(3, N, C, C)
    summed = lax.psum_scatter(
        terms.astype(jnp.bfloat16), "px", scatter_dimension=1, tiled=True
    ).astype(jnp.float32)
    summed = lax.psum_scatter(
        summed.astype(jnp.bfloat16), "py", scatter_dimension=2, tiled=True
    ).astype(jnp.float32)
    grad_taps = finish_taps(summed, own_log_terms(taps, count_px), count_py)
    return (mapped, grad_field, grad_taps)


def solution(mesh):
    count_px, count_py = mesh.shape["px"], mesh.shape["py"]
    fits = N * C == 128 * count_px * count_py and N == 8 * count_px and N == 16 * count_py
    spec = P(None, "px", "py", None)
    return jax.shard_map(
        plane_device if fits else line_device,
        mesh=mesh,
        in_specs=(spec, spec, P()),
        out_specs=(spec, spec, spec),
        check_vma=False,
    )
```

```python
import math

import jax
import jax.numpy as jnp
import numpy as np
from jax import lax
from jax.experimental import pallas as pl
from jax.experimental.pallas import tpu as pltpu
from jax.sharding import PartitionSpec as P

N = 64
C = 64
F32 = jnp.float32
BF16 = jnp.bfloat16


def real_dft(length):
    half = length // 2
    slot = np.arange(half)[:, None]
    at = np.arange(length)[None, :]
    angle = 2.0 * np.pi * ((slot * at) % length) / length
    real = np.cos(angle)
    imag = -np.sin(angle)
    imag[0] = (-1.0) ** np.arange(length)
    forward = np.concatenate([real, imag], 0)
    weight = np.where(np.arange(half) == 0, 1.0, 2.0) / length
    inverse = (forward * np.concatenate([weight, weight])[:, None]).T
    return forward, inverse


def line_table():
    at = np.arange(N)[None, :]
    freq = np.arange(N // 2 + 1)[:, None]
    angle = 2.0 * np.pi * ((freq * at) % N) / N
    return np.concatenate([np.cos(angle), -np.sin(angle[: N // 2]), np.zeros((7, N))], 0)


def pair_table():
    length = N // 2
    half = length // 2
    slot = np.arange(half)
    table = np.zeros((2, 2, 2, half, 2, N))
    for row in range(2):
        for col in range(2):
            for t in range((row + col) % 2, N, 2):
                lag = (t - col + row) // 2
                angle = 2.0 * np.pi * ((slot * lag) % length) / length
                cos, sin = np.cos(angle), np.sin(angle)
                other = cos.copy()
                other[0] = (-1.0) ** lag
                sin[0] = 0.0
                table[col, 0, 0, :, row, t] = cos
                table[col, 1, 1, :, row, t] = other
                table[col, 0, 1, :, row, t] = -sin
                table[col, 1, 0, :, row, t] = sin
    return table.reshape(8 * half, 2 * N)


def lag_rows(length, lag):
    half = length // 2
    slot = np.arange(half)
    angle = 2.0 * np.pi * ((slot * lag) % length) / length
    weight = np.where(slot == 0, 1.0, 2.0) / length
    real = np.cos(angle) * weight
    imag = np.sin(angle) * weight
    imag[0] = (-1.0) ** lag / length
    return np.concatenate([real, imag])


def tap_tables():
    scale = float(N) ** -1.5
    half = N // 2
    direct = np.stack([lag_rows(N, t) for t in range(N)], 0)
    paired = np.stack([np.concatenate([lag_rows(half, d), lag_rows(half, d + 1)]) for d in range(half)], 0)
    return direct * scale, paired * scale


def dot(a, b):
    return jnp.dot(a, b, preferred_element_type=F32)


def dot_nt(a, b):
    return lax.dot_general(a, b, (((1,), (1,)), ((), ())), preferred_element_type=F32)


def dot_tn(a, b):
    return lax.dot_general(a, b, (((0,), (0,)), ((), ())), preferred_element_type=F32)


def whole(count):
    return [pl.BlockSpec(memory_space=pltpu.VMEM)] * count


def params(megabytes):
    return pltpu.CompilerParams(vmem_limit_bytes=megabytes << 20)


def expand_to(out_ref, table_ref, row_of, col_of, row_lane, col_lane):
    size = out_ref.shape[0]
    small_rows, small_cols = table_ref.shape
    pick = lax.broadcasted_iota(jnp.int32, (small_cols, size), 0)
    wide = lax.broadcasted_iota(jnp.int32, (small_cols, size), 1)
    columns = jnp.where(pick == col_of(wide), 1.0, 0.0).astype(BF16)
    chunk = 256

    @pl.loop(0, size // chunk)
    def _(step):
        base = step * chunk
        tall = lax.broadcasted_iota(jnp.int32, (chunk, small_rows), 0) + base
        which = lax.broadcasted_iota(jnp.int32, (chunk, small_rows), 1)
        rows = jnp.where(row_of(tall) == which, 1.0, 0.0).astype(BF16)
        values = dot(dot(rows, table_ref[...]).astype(BF16), columns)
        at_row = lax.broadcasted_iota(jnp.int32, (chunk, size), 0) + base
        at_col = lax.broadcasted_iota(jnp.int32, (chunk, size), 1)
        keep = row_lane(at_row) == col_lane(at_col)
        out_ref[pl.ds(pl.multiple_of(base, chunk), chunk), :] = jnp.where(keep, values, 0.0).astype(BF16)


def high(v):
    return v // 16


def low(v):
    return v % 16


def y_position(v):
    return (v // 256) * 16 + v % 16


def y_lane(v):
    return (v // 16) % 16


def tables_kernel(fwd, inv, fwd_z, inv_z, fx, ix, fy, iy, fz, iz):
    expand_to(fz, fwd_z, high, high, low, low)
    expand_to(iz, inv_z, high, high, low, low)
    expand_to(fx, fwd, high, high, low, low)
    expand_to(ix, inv, high, high, low, low)
    expand_to(fy, fwd, high, y_position, low, y_lane)
    expand_to(iy, inv, y_position, high, y_lane, low)


def tables(fwd, inv, fwd_z, inv_z):
    big = jax.ShapeDtypeStruct((1024, 1024), BF16)
    small = jax.ShapeDtypeStruct((512, 512), BF16)
    return pl.pallas_call(
        tables_kernel,
        out_shape=(big, big, big, big, small, small),
        in_specs=whole(4),
        out_specs=tuple(whole(6)),
        compiler_params=params(40),
        cost_estimate=pl.CostEstimate(flops=2 << 30, bytes_accessed=12 << 20, transcendentals=0),
        name="tables",
    )(fwd, inv, fwd_z, inv_z)


def mixing_kernel(taps, e_line, e_pair, mix_x, mix_y, mix_z, wide, lines, pairs):
    row = lax.broadcasted_iota(jnp.int32, (64, 64, 64), 1)
    col = lax.broadcasted_iota(jnp.int32, (64, 64, 64), 2)
    for axis in range(3):
        masked = jnp.where(col <= row, taps[axis].astype(F32), 0.0).reshape(4096, 64)
        wide[:, :64] = masked
        wide[:, 64:] = jnp.zeros_like(masked)

        if axis < 2:
            out = mix_x if axis == 0 else mix_y

            @pl.loop(0, 64, unroll=8)
            def _(co):
                at = wide[pl.ds(co, 64, stride=64), :].astype(BF16)
                lines[pl.ds(co, 72, stride=64), :] = dot(e_line[...], at)

            @pl.loop(0, 32, unroll=4)
            def _(slot):
                def block(index):
                    one = lines[pl.ds(pl.multiple_of(index * 64, 64), 64), :]
                    return jnp.concatenate([one, pltpu.roll(one, 64, 1)], 0)

                imag = block(33 + slot)
                out[0, 0, slot] = block(slot).astype(BF16)
                out[1, 1, slot] = block(jnp.where(slot == 0, 32, slot)).astype(BF16)
                out[1, 0, slot] = imag.astype(BF16)
                out[0, 1, slot] = (-imag).astype(BF16)

        else:

            @pl.loop(0, 64, unroll=8)
            def _(co):
                at = wide[pl.ds(co, 64, stride=64), :]
                both = jnp.concatenate([at, pltpu.roll(at, 64, 1)], 0).astype(BF16)
                got = dot(e_pair[...], both)
                pairs[pl.ds(co, 64, stride=128), :] = got[:64]
                pairs[pl.ds(co + 64, 64, stride=128), :] = got[64:]

            for ri in range(2):
                for to in range(2):

                    @pl.loop(0, 16, unroll=4)
                    def _(slot):
                        start = ((ri * 2 + to) * 16 + slot) * 128
                        mix_z[to, ri, slot] = pairs[pl.ds(pl.multiple_of(start, 128), 128), :].astype(BF16)


def mixing(taps, e_line, e_pair):
    line = jax.ShapeDtypeStruct((2, 2, 32, 128, 128), BF16)
    pair = jax.ShapeDtypeStruct((2, 2, 16, 128, 128), BF16)
    return pl.pallas_call(
        mixing_kernel,
        out_shape=(line, line, pair),
        in_specs=whole(3),
        out_specs=tuple(whole(3)),
        scratch_shapes=[
            pltpu.VMEM((4096, 128), F32),
            pltpu.VMEM((72 * 64, 128), F32),
            pltpu.VMEM((64 * 128, 128), F32),
        ],
        compiler_params=params(40),
        cost_estimate=pl.CostEstimate(flops=2 << 30, bytes_accessed=12 << 20, transcendentals=0),
        name="mixing",
    )(taps, e_line, e_pair)


def mix_matrix(mix_ref, slot):
    top = jnp.concatenate([mix_ref[0, 0, slot], mix_ref[0, 1, slot]], 1)
    bottom = jnp.concatenate([mix_ref[1, 0, slot], mix_ref[1, 1, slot]], 1)
    return jnp.concatenate([top, bottom], 0)


def mix_apply(val, matrix, adjoint):
    return (dot(val, matrix) if adjoint else dot_nt(val, matrix)).astype(BF16)


def gradient_blocks(cot, val, slot):
    outer = dot_tn(cot, val)
    first = slot == 0
    real_real = outer[:128, :128]
    imag_imag = outer[128:, 128:]
    crossed = outer[:128, 128:] - outer[128:, :128]
    real = jnp.where(first, real_real, real_real + imag_imag)
    imag = jnp.where(first, imag_imag, crossed)
    return real, imag


def to_lags(table, sums, out):
    lags, depth = table.shape

    @pl.loop(0, 64, unroll=8)
    def _(co):
        rows = sums[pl.ds(co, depth, stride=64), :]
        out[pl.ds(co, lags, stride=64), :] = jnp.dot(
            table[...], rows, preferred_element_type=F32, precision=lax.Precision.HIGHEST
        )


def line_pass(axis, adjoint, values, fwd, inv, mix, out, spec, mixed, rhs, accumulate=None):
    @pl.loop(0, 4)
    def _(j):
        for h in range(2):
            block = values[:, j, h] if axis == "x" else values[2 * j + h]
            rhs[:, h * 128 : (h + 1) * 128] = block.reshape(1024, 128)
        for ri in range(2):
            for part in range(2):
                start = ri * 512 + part * 256
                got = dot(fwd[start : start + 256, :], rhs[...]).astype(BF16).reshape(16, 16, 256)
                for h in range(2):
                    spec[part * 16 : (part + 1) * 16, 2 * j + h, :, ri * 128 : (ri + 1) * 128] = got[
                        :, :, h * 128 : (h + 1) * 128
                    ]

    @pl.loop(0, 32, unroll=4)
    def _(slot):
        val = spec[slot].reshape(128, 256)
        mixed[slot] = mix_apply(val, mix_matrix(mix, slot), adjoint).reshape(8, 16, 256)
        if accumulate is not None:
            accumulate(slot, val)

    @pl.loop(0, 4)
    def _(j):
        for h in range(2):
            for ri in range(2):
                rhs[ri * 512 : (ri + 1) * 512, h * 128 : (h + 1) * 128] = mixed[
                    :, 2 * j + h, :, ri * 128 : (ri + 1) * 128
                ].reshape(512, 128)
        for part in range(4):
            got = dot(inv[part * 256 : (part + 1) * 256, :], rhs[...]).astype(BF16)
            for h in range(2):
                piece = got[:, h * 128 : (h + 1) * 128].reshape(2, 8, 16, 128)
                if axis == "x":
                    out[part * 2 : (part + 1) * 2, j, h] = piece
                else:
                    out[2 * j + h, part] = piece


def planes_adjoint_kernel(values, fx, ix, fy, iy, mix_x, mix_y, out, spec_x, spec_y, between, mixed, rhs):
    line_pass("x", True, values, fx, ix, mix_x, between, spec_x, mixed, rhs)
    line_pass("y", True, between, fy, iy, mix_y, out, spec_y, mixed, rhs)


def planes_kernel(
    values, fx, ix, fy, iy, mix_x, mix_y, cot_x, cot_y, table, out, terms, between, spec, mixed, rhs, sums
):
    lane = lax.broadcasted_iota(jnp.int32, (64, 128), 1)

    def add_y(slot, val):
        blocks = gradient_blocks(cot_y[slot].reshape(128, 256), val, slot)
        for ri in range(2):
            at = pl.ds(pl.multiple_of((ri * 32 + slot) * 64, 64), 64)
            sums[at, :] = blocks[ri][64:] + pltpu.roll(blocks[ri][:64], 64, 1)

    def add_x(slot, val):
        blocks = gradient_blocks(cot_x[slot].reshape(128, 256), val, slot)
        for ri in range(2):
            at = pl.ds(pl.multiple_of((ri * 32 + slot) * 64, 64), 64)
            got = blocks[ri][:64] + pltpu.roll(blocks[ri][64:], 64, 1)
            sums[at, :] = jnp.where(lane < 64, got, sums[at, :])

    line_pass("y", False, values, fy, iy, mix_y, between, spec, mixed, rhs, add_y)
    line_pass("x", False, between, fx, ix, mix_x, out, spec, mixed, rhs, add_x)
    to_lags(table, sums, terms)


SPEC = (32, 8, 16, 256)


def planes_adjoint(values, fx, ix, fy, iy, mix_x, mix_y):
    spec = jax.ShapeDtypeStruct(SPEC, BF16)
    return pl.pallas_call(
        planes_adjoint_kernel,
        out_shape=(jax.ShapeDtypeStruct(values.shape, BF16), spec, spec),
        in_specs=whole(7),
        out_specs=tuple(whole(3)),
        scratch_shapes=[
            pltpu.VMEM(values.shape, BF16),
            pltpu.VMEM(SPEC, BF16),
            pltpu.VMEM((1024, 256), BF16),
        ],
        compiler_params=params(44),
        cost_estimate=pl.CostEstimate(flops=10 << 30, bytes_accessed=24 << 20, transcendentals=0),
        name="planes_adjoint",
    )(values, fx, ix, fy, iy, mix_x, mix_y)


def planes(values, fx, ix, fy, iy, mix_x, mix_y, cot_x, cot_y, table):
    return pl.pallas_call(
        planes_kernel,
        out_shape=(
            jax.ShapeDtypeStruct(values.shape, BF16),
            jax.ShapeDtypeStruct((4096, 128), F32),
        ),
        in_specs=whole(10),
        out_specs=tuple(whole(2)),
        scratch_shapes=[
            pltpu.VMEM(values.shape, BF16),
            pltpu.VMEM(SPEC, BF16),
            pltpu.VMEM(SPEC, BF16),
            pltpu.VMEM((1024, 256), BF16),
            pltpu.VMEM((4096, 128), F32),
        ],
        compiler_params=params(44),
        cost_estimate=pl.CostEstimate(flops=12 << 30, bytes_accessed=28 << 20, transcendentals=0),
        name="planes",
    )(values, fx, ix, fy, iy, mix_x, mix_y, cot_x, cot_y, table)


def depth_forward(adjoint, values, fwd, spec, rhs):
    @pl.loop(0, 8)
    def _(j):
        for h in range(2):
            lanes = slice(h * 128, (h + 1) * 128)
            if adjoint:
                rhs[:, lanes] = values[:, 2 * j + h].reshape(512, 128)
            else:
                for zp in range(32):
                    rhs[zp * 16 : (zp + 1) * 16, lanes] = values[2 * j + h, :, zp * 128 : (zp + 1) * 128]
        for ri in range(2):
            got = dot(fwd[ri * 256 : (ri + 1) * 256, :], rhs[...]).astype(BF16).reshape(16, 16, 256)
            for h in range(2):
                spec[:, 2 * j + h, :, ri * 128 : (ri + 1) * 128] = got[:, :, h * 128 : (h + 1) * 128]


def depth_backward(adjoint, spec, inv, mix, out, mixed, rhs):
    @pl.loop(0, 16, unroll=4)
    def _(slot):
        val = spec[slot].reshape(256, 256)
        mixed[slot] = mix_apply(val, mix_matrix(mix, slot), adjoint).reshape(16, 16, 256)

    @pl.loop(0, 8)
    def _(j):
        for h in range(2):
            for ri in range(2):
                rhs[ri * 256 : (ri + 1) * 256, h * 128 : (h + 1) * 128] = mixed[
                    :, 2 * j + h, :, ri * 128 : (ri + 1) * 128
                ].reshape(256, 128)
        for part in range(2):
            got = dot(inv[part * 256 : (part + 1) * 256, :], rhs[...]).astype(BF16)
            for h in range(2):
                lanes = slice(h * 128, (h + 1) * 128)
                if adjoint:
                    for zp in range(16):
                        place = (part * 16 + zp) * 128
                        out[2 * j + h, :, place : place + 128] = got[zp * 16 : (zp + 1) * 16, lanes]
                else:
                    out[part * 16 : (part + 1) * 16, 2 * j + h] = got[:, lanes].reshape(16, 16, 128)


DEPTH_SPEC = (16, 16, 16, 256)


def depth_kernel(values, fwd, inv, mix, out, spec, mixed, rhs):
    depth_forward(False, values, fwd, spec, rhs)
    depth_backward(False, spec, inv, mix, out, mixed, rhs)


def depth_sums_kernel(values, fwd, other, table, spec, terms, rhs, sums):
    lane = lax.broadcasted_iota(jnp.int32, (64, 128), 1)

    depth_forward(True, values, fwd, spec, rhs)

    @pl.loop(0, 16, unroll=4)
    def _(slot):
        val = spec[slot].reshape(256, 256)
        blocks = gradient_blocks(val, other[slot].reshape(256, 256), slot)
        for ri in range(2):
            top, bottom = blocks[ri][:64], pltpu.roll(blocks[ri][64:], 64, 1)
            at = pl.multiple_of((ri * 16 + slot) * 64, 64)
            sums[pl.ds(at, 64), :] = jnp.where(lane < 64, top, 0.0) + bottom
            sums[pl.ds(at + 2048, 64), :] = jnp.where(lane < 64, 0.0, top)

    to_lags(table, sums, terms)


def depth_adjoint_kernel(spec, inv, mix, out, mixed, rhs):
    depth_backward(True, spec, inv, mix, out, mixed, rhs)


def depth(values, fwd, inv, mix):
    return pl.pallas_call(
        depth_kernel,
        out_shape=(
            jax.ShapeDtypeStruct((32, 16, 16, 128), BF16),
            jax.ShapeDtypeStruct(DEPTH_SPEC, BF16),
        ),
        in_specs=whole(4),
        out_specs=tuple(whole(2)),
        scratch_shapes=[pltpu.VMEM(DEPTH_SPEC, BF16), pltpu.VMEM((512, 256), BF16)],
        compiler_params=params(24),
        cost_estimate=pl.CostEstimate(flops=4 << 30, bytes_accessed=10 << 20, transcendentals=0),
        name="depth",
    )(values, fwd, inv, mix)


def depth_sums(values, fwd, other, table):
    return pl.pallas_call(
        depth_sums_kernel,
        out_shape=(
            jax.ShapeDtypeStruct(DEPTH_SPEC, BF16),
            jax.ShapeDtypeStruct((2048, 128), F32),
        ),
        in_specs=whole(4),
        out_specs=tuple(whole(2)),
        scratch_shapes=[pltpu.VMEM((512, 256), BF16), pltpu.VMEM((4096, 128), F32)],
        compiler_params=params(58),
        cost_estimate=pl.CostEstimate(flops=4 << 30, bytes_accessed=8 << 20, transcendentals=0),
        name="depth_sums",
    )(values, fwd, other, table)


def depth_adjoint(spec, inv, mix):
    return pl.pallas_call(
        depth_adjoint_kernel,
        out_shape=jax.ShapeDtypeStruct((16, 16, 4096), BF16),
        in_specs=whole(3),
        out_specs=whole(1)[0],
        scratch_shapes=[pltpu.VMEM(DEPTH_SPEC, BF16), pltpu.VMEM((512, 256), BF16)],
        compiler_params=params(24),
        cost_estimate=pl.CostEstimate(flops=2 << 30, bytes_accessed=6 << 20, transcendentals=0),
        name="depth_adjoint",
    )(spec, inv, mix)


def to_pairs_kernel(src, dst, wide, narrow, came, went):
    arrivals = [pltpu.make_async_copy(src.at[k], wide.at[k], came.at[k]) for k in range(4)]
    departures = [pltpu.make_async_copy(narrow.at[k], dst.at[:, k], went.at[k]) for k in range(4)]
    for copy in arrivals:
        copy.start()
    for k in range(4):
        arrivals[k].wait()
        for zp in range(32):
            narrow[k, zp] = wide[k, :, :, zp * 128 : (zp + 1) * 128]
        departures[k].start()
    for copy in departures:
        copy.wait()


def to_pairs(columns):
    return pl.pallas_call(
        to_pairs_kernel,
        out_shape=jax.ShapeDtypeStruct((32, 4, 4, 16, 128), BF16),
        in_specs=[pl.BlockSpec(memory_space=pltpu.HBM)],
        out_specs=pl.BlockSpec(memory_space=pltpu.HBM),
        scratch_shapes=[
            pltpu.VMEM((4, 4, 16, 4096), BF16),
            pltpu.VMEM((4, 32, 4, 16, 128), BF16),
            pltpu.SemaphoreType.DMA((4,)),
            pltpu.SemaphoreType.DMA((4,)),
        ],
        compiler_params=params(60),
        cost_estimate=pl.CostEstimate(flops=0, bytes_accessed=4 << 20, transcendentals=0),
        name="to_pairs",
    )(columns.reshape(4, 4, 16, 4096)).reshape(32, 16, 16, 128)


def from_pairs_kernel(src, dst, wide, went):
    departures = [pltpu.make_async_copy(wide.at[k], dst.at[k], went.at[k]) for k in range(4)]
    for k in range(4):
        for zp in range(32):
            wide[k, :, :, zp * 128 : (zp + 1) * 128] = src[zp, k]
        departures[k].start()
    for copy in departures:
        copy.wait()


def from_pairs(pairs):
    return pl.pallas_call(
        from_pairs_kernel,
        out_shape=jax.ShapeDtypeStruct((4, 4, 16, 4096), BF16),
        in_specs=whole(1),
        out_specs=pl.BlockSpec(memory_space=pltpu.HBM),
        scratch_shapes=[pltpu.VMEM((4, 4, 16, 4096), BF16), pltpu.SemaphoreType.DMA((4,))],
        compiler_params=params(8),
        cost_estimate=pl.CostEstimate(flops=0, bytes_accessed=4 << 20, transcendentals=0),
        name="from_pairs",
    )(pairs.reshape(32, 4, 4, 16, 128))


def dft_tables(row_ids, col_ids, length):
    product = row_ids[:, None] * col_ids[None, :] % length
    angle = product.astype(jnp.float32) * (2.0 * math.pi / length)
    return (jnp.cos(angle), jnp.sin(angle))


def log_terms(taps, row_ids, col_ids, length):
    highest = lax.Precision.HIGHEST
    diag_w = jnp.diagonal(taps.astype(jnp.float32), axis1=2, axis2=3)
    cos_full, sin_full = dft_tables(row_ids, row_ids, length)
    real_z = jnp.einsum("kt,atc->akc", cos_full, diag_w, precision=highest)
    imag_z = -jnp.einsum("kt,atc->akc", sin_full, diag_w, precision=highest)
    modulus = real_z * real_z + imag_z * imag_z
    cos_cols, sin_cols = dft_tables(row_ids, col_ids, length)
    summed = jnp.einsum("kt,akc->atc", cos_cols, real_z / modulus, precision=highest) - jnp.einsum(
        "kt,akc->atc", sin_cols, imag_z / modulus, precision=highest
    )
    return summed / math.sqrt(length)


def own_log_terms(taps, count_px):
    all_ids = jnp.arange(N, dtype=jnp.int32)
    slab_t = N // count_px
    t_ids = lax.axis_index("px") * slab_t + jnp.arange(slab_t, dtype=jnp.int32)
    return log_terms(taps, all_ids, t_ids, N)


def finish_taps(summed, log_part, count_py):
    slab_o = C // count_py
    o_ids = lax.axis_index("py") * slab_o + jnp.arange(slab_o, dtype=jnp.int32)
    channel_ids = jnp.arange(C, dtype=jnp.int32)
    diagonal_sel = (channel_ids[None, :] == o_ids[:, None]).astype(jnp.float32)
    keep_mask = (channel_ids[None, :] <= o_ids[:, None]).astype(jnp.float32)
    return keep_mask * (summed - log_part[:, :, None, :] * diagonal_sel)


def halve(values, dim, axis, bit):
    count = lax.axis_size(axis)
    mine = (lax.axis_index(axis) >> bit) & 1
    keep = lax.dynamic_index_in_dim(values, mine, dim, keepdims=False)
    send = lax.dynamic_index_in_dim(values, 1 - mine, dim, keepdims=False).astype(BF16)
    got = lax.ppermute(send, axis, [(i, i ^ (1 << bit)) for i in range(count)])
    return keep + got.astype(F32)


def plane_device(field, cotangent, taps):
    axes = ("px", "py")
    count_px = lax.axis_size("px")
    count_py = lax.axis_size("py")
    shape = field.shape
    count = count_px * count_py
    column_shape = (count, 16, 16, 128)
    plane_shape = (count_px, count_py, 2, 8, 16, 128)

    def exchange(values):
        return lax.all_to_all(values, axes, 0, 0, tiled=True)

    cot_planes = exchange(to_pairs(cotangent.reshape(16, 16, 4096))).reshape(plane_shape)

    small = real_dft(N) + real_dft(N // 2)
    fx, ix, fy, iy, fz, iz = tables(*[jnp.asarray(v, BF16) for v in small])
    mix_x, mix_y, mix_z = mixing(taps, jnp.asarray(line_table(), BF16), jnp.asarray(pair_table(), BF16))
    direct, paired = [jnp.asarray(v, F32) for v in tap_tables()]

    first, field_spec = depth(field.reshape(16, 16, 4096), fz, iz, mix_z)
    first_planes = exchange(first).reshape(plane_shape)

    fx_then, log_part = lax.optimization_barrier((fx, own_log_terms(taps, count_px)))
    back_one, cot_spec, back_spec = planes_adjoint(cot_planes, fx_then, ix, fy, iy, mix_x, mix_y)
    back_columns = exchange(back_one.reshape(column_shape))

    out, terms_xy = planes(first_planes, fx, ix, fy, iy, mix_x, mix_y, cot_spec, back_spec, direct)
    out_columns = exchange(out.reshape(column_shape))

    def split(terms, rows):
        return halve(terms.reshape(2, 2, 2, rows, 2, 2, 16, 128), 5, "py", 0)

    terms_xy = split(terms_xy, 8)
    terms_xy = halve(terms_xy, 4, "py", 1)

    back_hat, terms_z = depth_sums(back_columns, fz, field_spec, paired)
    mapped = from_pairs(out_columns).reshape(shape)

    terms_z = split(terms_z, 4)
    terms_z, back_hat = lax.optimization_barrier((terms_z, back_hat))
    terms_z = halve(terms_z, 4, "py", 1)
    grad_field = depth_adjoint(back_hat, iz, mix_z)
    terms_z, grad_field = lax.optimization_barrier((terms_z, grad_field))
    terms = jnp.concatenate([terms_xy, terms_z], 3)
    for dim, bit in ((2, 0), (1, 1), (0, 2)):
        terms = halve(terms, dim, "px", bit)
    along_z = terms[8:].reshape(4, 16, 2, C).transpose(0, 2, 1, 3).reshape(8, 16, C)
    summed = jnp.stack([terms[:8, :, :C], terms[:8, :, C:], along_z], 0)
    grad_taps = finish_taps(summed, log_part, count_py)
    return (mapped, grad_field.reshape(shape), grad_taps)


def along(values, table, position):
    letters = "abcdef"[: values.ndim]
    target = letters[:position] + "k" + letters[position + 1 :]
    return jnp.einsum(
        letters + ",k" + letters[position] + "->" + target,
        values,
        table,
        preferred_element_type=jnp.float32,
    )


def section(values, position, cos_b, sin_b, turn_sign, factor):
    direct = along(values, cos_b, position)
    crossed = along(values, sin_b, position)
    half = values.shape[-1] // 2
    turned = jnp.concatenate([crossed[..., half:], -crossed[..., :half]], -1)
    return ((direct + turn_sign * turned) * factor).astype(jnp.bfloat16)


def z_forward(values, cos_b, sin_b):
    direct = along(values, cos_b, 3)
    crossed = along(values, sin_b, 3)
    return jnp.concatenate([direct, -crossed], -1).astype(jnp.bfloat16)


def z_inverse(values, cos_b, sin_b, factor):
    half = values.shape[-1] // 2
    real_part = along(values[..., :half], cos_b, 3)
    imag_part = along(values[..., half:], sin_b, 3)
    return ((real_part - imag_part) * factor).astype(jnp.bfloat16)


def spectra(taps_axis, cos_b, sin_b):
    real_w = jnp.einsum("kt,toi->koi", cos_b, taps_axis, preferred_element_type=jnp.float32)
    imag_w = -jnp.einsum("kt,toi->koi", sin_b, taps_axis, preferred_element_type=jnp.float32)
    upper = jnp.concatenate([real_w, -imag_w], 2)
    lower = jnp.concatenate([imag_w, real_w], 2)
    return jnp.concatenate([upper, lower], 1).astype(jnp.bfloat16)


def push(values, matrix, position):
    letters = "abcde"
    return jnp.einsum(
        letters + "," + letters[position] + "fe->abcdf",
        values,
        matrix,
        preferred_element_type=jnp.float32,
    ).astype(jnp.bfloat16)


def pull(values, matrix, position):
    letters = "abcde"
    return jnp.einsum(
        letters + "," + letters[position] + "ef->abcdf",
        values,
        matrix,
        preferred_element_type=jnp.float32,
    ).astype(jnp.bfloat16)


def outer(left, right, position):
    letters = "abcde"
    return jnp.einsum(
        "abcde,abcdf->" + letters[position] + "ef", left, right, preferred_element_type=jnp.float32
    )


def tap_terms(spectral, cos_f, sin_f, split_t, split_o):
    width = spectral.shape[1] // 2
    count = spectral.shape[0]
    real_g = spectral[:, :width, :width] + spectral[:, width:, width:]
    imag_g = spectral[:, :width, width:] - spectral[:, width:, :width]
    cos_r = cos_f.reshape(count, split_t, -1)
    sin_r = sin_f.reshape(count, split_t, -1)
    real_r = real_g.reshape(count, split_o, -1, width)
    imag_r = imag_g.reshape(count, split_o, -1, width)
    highest = lax.Precision.HIGHEST
    return jnp.einsum("kpu,kqvi->pquvi", cos_r, real_r, precision=highest) + jnp.einsum(
        "kpu,kqvi->pquvi", sin_r, imag_r, precision=highest
    )


def line_device(field, cotangent, taps):
    batch_rows = field.shape[0]
    local_x = field.shape[1]
    local_y = field.shape[2]
    count_px = lax.axis_size("px")
    count_py = lax.axis_size("py")
    all_ids = jnp.arange(N, dtype=jnp.int32)
    cos_f, sin_f = dft_tables(all_ids, all_ids, N)
    cos_b = cos_f.astype(jnp.bfloat16)
    sin_b = sin_f.astype(jnp.bfloat16)
    stacked = jnp.concatenate([field, cotangent], 0).reshape(2 * batch_rows, local_x, local_y, N, C)
    spectral = z_forward(stacked, cos_b, sin_b)
    spectral = section(
        lax.all_to_all(spectral, "py", split_axis=3, concat_axis=2, tiled=True),
        2,
        cos_b,
        sin_b,
        1.0,
        1.0,
    )
    spectral = section(
        lax.all_to_all(spectral, "px", split_axis=2, concat_axis=1, tiled=True),
        1,
        cos_b,
        sin_b,
        1.0,
        1.0,
    )
    field_hat = spectral[:batch_rows]
    cot_hat = spectral[batch_rows:]
    count_ky = N // count_px
    count_kz = N // count_py
    ky_ids = lax.axis_index("px") * count_ky + jnp.arange(count_ky, dtype=jnp.int32)
    kz_ids = lax.axis_index("py") * count_kz + jnp.arange(count_kz, dtype=jnp.int32)
    cos_y, sin_y = dft_tables(ky_ids, all_ids, N)
    cos_z, sin_z = dft_tables(kz_ids, all_ids, N)
    lower_mask = jnp.tril(jnp.ones((C, C), jnp.float32))
    masked = (taps.astype(jnp.float32) * lower_mask).astype(jnp.bfloat16)
    mix_x = spectra(masked[0], cos_b, sin_b)
    mix_y = spectra(masked[1], cos_y.astype(jnp.bfloat16), sin_y.astype(jnp.bfloat16))
    mix_z = spectra(masked[2], cos_z.astype(jnp.bfloat16), sin_z.astype(jnp.bfloat16))
    first = push(field_hat, mix_z, 3)
    second = push(first, mix_y, 2)
    out_hat = push(second, mix_x, 1)
    back_two = pull(cot_hat, mix_x, 1)
    back_one = pull(back_two, mix_y, 2)
    back_hat = pull(back_one, mix_z, 3)
    grad_x_spec = outer(cot_hat, second, 1)
    grad_y_spec = outer(back_two, first, 2)
    grad_z_spec = outer(back_one, field_hat, 3)
    returned = section(jnp.concatenate([out_hat, back_hat], 0), 1, cos_b, sin_b, -1.0, 1.0 / N)
    returned = section(
        lax.all_to_all(returned, "px", split_axis=1, concat_axis=2, tiled=True),
        2,
        cos_b,
        sin_b,
        -1.0,
        1.0 / N,
    )
    returned = z_inverse(
        lax.all_to_all(returned, "py", split_axis=2, concat_axis=3, tiled=True),
        cos_b,
        sin_b,
        1.0 / N,
    )
    returned = returned.reshape(2 * batch_rows, local_x, local_y, N * C)
    mapped = returned[:batch_rows]
    grad_field = returned[batch_rows:]
    data_scale = 1.0 / (float(N) ** 4 * math.sqrt(N))
    terms = (
        jnp.stack(
            [
                tap_terms(grad_x_spec, cos_f, sin_f, 1, 1),
                tap_terms(grad_y_spec, cos_y, sin_y, 1, 1),
                tap_terms(grad_z_spec, cos_z, sin_z, 1, 1),
            ],
            2,
        )
        * data_scale
    ).reshape(3, N, C, C)
    summed = lax.psum_scatter(
        terms.astype(jnp.bfloat16), "px", scatter_dimension=1, tiled=True
    ).astype(jnp.float32)
    summed = lax.psum_scatter(
        summed.astype(jnp.bfloat16), "py", scatter_dimension=2, tiled=True
    ).astype(jnp.float32)
    grad_taps = finish_taps(summed, own_log_terms(taps, count_px), count_py)
    return (mapped, grad_field, grad_taps)


def solution(mesh):
    count_px, count_py = mesh.shape["px"], mesh.shape["py"]
    fits = N * C == 128 * count_px * count_py and N == 8 * count_px and N == 16 * count_py
    spec = P(None, "px", "py", None)
    return jax.shard_map(
        plane_device if fits else line_device,
        mesh=mesh,
        in_specs=(spec, spec, P()),
        out_specs=(spec, spec, spec),
        check_vma=False,
    )
```

```python
import math

import jax
import jax.numpy as jnp
import numpy as np
from jax import lax
from jax.experimental import pallas as pl
from jax.experimental.pallas import tpu as pltpu
from jax.sharding import PartitionSpec as P

N = 64
C = 64
F32 = jnp.float32
BF16 = jnp.bfloat16


def real_dft(length):
    half = length // 2
    slot = np.arange(half)[:, None]
    at = np.arange(length)[None, :]
    angle = 2.0 * np.pi * ((slot * at) % length) / length
    real = np.cos(angle)
    imag = -np.sin(angle)
    imag[0] = (-1.0) ** np.arange(length)
    forward = np.concatenate([real, imag], 0)
    weight = np.where(np.arange(half) == 0, 1.0, 2.0) / length
    inverse = (forward * np.concatenate([weight, weight])[:, None]).T
    return forward, inverse


def line_table():
    at = np.arange(N)[None, :]
    freq = np.arange(N // 2 + 1)[:, None]
    angle = 2.0 * np.pi * ((freq * at) % N) / N
    return np.concatenate([np.cos(angle), -np.sin(angle[: N // 2]), np.zeros((7, N))], 0)


def pair_table():
    length = N // 2
    half = length // 2
    slot = np.arange(half)
    table = np.zeros((2, 2, 2, half, 2, N))
    for row in range(2):
        for col in range(2):
            for t in range((row + col) % 2, N, 2):
                lag = (t - col + row) // 2
                angle = 2.0 * np.pi * ((slot * lag) % length) / length
                cos, sin = np.cos(angle), np.sin(angle)
                other = cos.copy()
                other[0] = (-1.0) ** lag
                sin[0] = 0.0
                table[col, 0, 0, :, row, t] = cos
                table[col, 1, 1, :, row, t] = other
                table[col, 0, 1, :, row, t] = -sin
                table[col, 1, 0, :, row, t] = sin
    return table.reshape(8 * half, 2 * N)


def lag_rows(length, lag):
    half = length // 2
    slot = np.arange(half)
    angle = 2.0 * np.pi * ((slot * lag) % length) / length
    weight = np.where(slot == 0, 1.0, 2.0) / length
    real = np.cos(angle) * weight
    imag = np.sin(angle) * weight
    imag[0] = (-1.0) ** lag / length
    return np.concatenate([real, imag])


def tap_tables():
    scale = float(N) ** -1.5
    half = N // 2
    direct = np.stack([lag_rows(N, t) for t in range(N)], 0)
    paired = np.stack([np.concatenate([lag_rows(half, d), lag_rows(half, d + 1)]) for d in range(half)], 0)
    return direct * scale, paired * scale


def dot(a, b):
    return jnp.dot(a, b, preferred_element_type=F32)


def dot_nt(a, b):
    return lax.dot_general(a, b, (((1,), (1,)), ((), ())), preferred_element_type=F32)


def dot_tn(a, b):
    return lax.dot_general(a, b, (((0,), (0,)), ((), ())), preferred_element_type=F32)


def whole(count):
    return [pl.BlockSpec(memory_space=pltpu.VMEM)] * count


def params(megabytes):
    return pltpu.CompilerParams(vmem_limit_bytes=megabytes << 20)


def expand_to(out_ref, table_ref, row_of, col_of, row_lane, col_lane):
    size = out_ref.shape[0]
    small_rows, small_cols = table_ref.shape
    pick = lax.broadcasted_iota(jnp.int32, (small_cols, size), 0)
    wide = lax.broadcasted_iota(jnp.int32, (small_cols, size), 1)
    columns = jnp.where(pick == col_of(wide), 1.0, 0.0).astype(BF16)
    chunk = 256

    @pl.loop(0, size // chunk)
    def _(step):
        base = step * chunk
        tall = lax.broadcasted_iota(jnp.int32, (chunk, small_rows), 0) + base
        which = lax.broadcasted_iota(jnp.int32, (chunk, small_rows), 1)
        rows = jnp.where(row_of(tall) == which, 1.0, 0.0).astype(BF16)
        values = dot(dot(rows, table_ref[...]).astype(BF16), columns)
        at_row = lax.broadcasted_iota(jnp.int32, (chunk, size), 0) + base
        at_col = lax.broadcasted_iota(jnp.int32, (chunk, size), 1)
        keep = row_lane(at_row) == col_lane(at_col)
        out_ref[pl.ds(pl.multiple_of(base, chunk), chunk), :] = jnp.where(keep, values, 0.0).astype(BF16)


def high(v):
    return v // 16


def low(v):
    return v % 16


def y_position(v):
    return (v // 256) * 16 + v % 16


def y_lane(v):
    return (v // 16) % 16


def tables_kernel(fwd, inv, fwd_z, inv_z, fx, ix, fy, iy, fz, iz):
    expand_to(fz, fwd_z, high, high, low, low)
    expand_to(iz, inv_z, high, high, low, low)
    expand_to(fx, fwd, high, high, low, low)
    expand_to(ix, inv, high, high, low, low)
    expand_to(fy, fwd, high, y_position, low, y_lane)
    expand_to(iy, inv, y_position, high, y_lane, low)


def tables(fwd, inv, fwd_z, inv_z):
    big = jax.ShapeDtypeStruct((1024, 1024), BF16)
    small = jax.ShapeDtypeStruct((512, 512), BF16)
    return pl.pallas_call(
        tables_kernel,
        out_shape=(big, big, big, big, small, small),
        in_specs=whole(4),
        out_specs=tuple(whole(6)),
        compiler_params=params(40),
        cost_estimate=pl.CostEstimate(flops=2 << 30, bytes_accessed=12 << 20, transcendentals=0),
        name="tables",
    )(fwd, inv, fwd_z, inv_z)


def mixing_kernel(taps, e_line, e_pair, mix_x, mix_y, mix_z, wide, lines, pairs):
    row = lax.broadcasted_iota(jnp.int32, (64, 64, 64), 1)
    col = lax.broadcasted_iota(jnp.int32, (64, 64, 64), 2)
    for axis in range(3):
        masked = jnp.where(col <= row, taps[axis].astype(F32), 0.0).reshape(4096, 64)
        wide[:, :64] = masked
        wide[:, 64:] = jnp.zeros_like(masked)

        if axis < 2:
            out = mix_x if axis == 0 else mix_y

            @pl.loop(0, 64, unroll=8)
            def _(co):
                at = wide[pl.ds(co, 64, stride=64), :].astype(BF16)
                lines[pl.ds(co, 72, stride=64), :] = dot(e_line[...], at)

            @pl.loop(0, 32, unroll=4)
            def _(slot):
                def block(index):
                    one = lines[pl.ds(pl.multiple_of(index * 64, 64), 64), :]
                    return jnp.concatenate([one, pltpu.roll(one, 64, 1)], 0)

                imag = block(33 + slot)
                out[0, 0, slot] = block(slot).astype(BF16)
                out[1, 1, slot] = block(jnp.where(slot == 0, 32, slot)).astype(BF16)
                out[1, 0, slot] = imag.astype(BF16)
                out[0, 1, slot] = (-imag).astype(BF16)

        else:

            @pl.loop(0, 64, unroll=8)
            def _(co):
                at = wide[pl.ds(co, 64, stride=64), :]
                both = jnp.concatenate([at, pltpu.roll(at, 64, 1)], 0).astype(BF16)
                got = dot(e_pair[...], both)
                pairs[pl.ds(co, 64, stride=128), :] = got[:64]
                pairs[pl.ds(co + 64, 64, stride=128), :] = got[64:]

            for ri in range(2):
                for to in range(2):

                    @pl.loop(0, 16, unroll=4)
                    def _(slot):
                        start = ((ri * 2 + to) * 16 + slot) * 128
                        mix_z[to, ri, slot] = pairs[pl.ds(pl.multiple_of(start, 128), 128), :].astype(BF16)


def mixing(taps, e_line, e_pair):
    line = jax.ShapeDtypeStruct((2, 2, 32, 128, 128), BF16)
    pair = jax.ShapeDtypeStruct((2, 2, 16, 128, 128), BF16)
    return pl.pallas_call(
        mixing_kernel,
        out_shape=(line, line, pair),
        in_specs=whole(3),
        out_specs=tuple(whole(3)),
        scratch_shapes=[
            pltpu.VMEM((4096, 128), F32),
            pltpu.VMEM((72 * 64, 128), F32),
            pltpu.VMEM((64 * 128, 128), F32),
        ],
        compiler_params=params(40),
        cost_estimate=pl.CostEstimate(flops=2 << 30, bytes_accessed=12 << 20, transcendentals=0),
        name="mixing",
    )(taps, e_line, e_pair)


def mix_matrix(mix_ref, slot):
    top = jnp.concatenate([mix_ref[0, 0, slot], mix_ref[0, 1, slot]], 1)
    bottom = jnp.concatenate([mix_ref[1, 0, slot], mix_ref[1, 1, slot]], 1)
    return jnp.concatenate([top, bottom], 0)


def mix_apply(val, matrix, adjoint):
    return (dot(val, matrix) if adjoint else dot_nt(val, matrix)).astype(BF16)


def gradient_blocks(cot, val, slot):
    outer = dot_tn(cot, val)
    first = slot == 0
    real_real = outer[:128, :128]
    imag_imag = outer[128:, 128:]
    crossed = outer[:128, 128:] - outer[128:, :128]
    real = jnp.where(first, real_real, real_real + imag_imag)
    imag = jnp.where(first, imag_imag, crossed)
    return real, imag


def to_lags(table, sums, out):
    lags, depth = table.shape

    @pl.loop(0, 64, unroll=8)
    def _(co):
        rows = sums[pl.ds(co, depth, stride=64), :]
        out[pl.ds(co, lags, stride=64), :] = jnp.dot(
            table[...], rows, preferred_element_type=F32, precision=lax.Precision.HIGHEST
        )


def line_pass(axis, adjoint, values, fwd, inv, mix, out, spec, mixed, rhs, accumulate=None):
    @pl.loop(0, 4)
    def _(j):
        for h in range(2):
            block = values[:, j, h] if axis == "x" else values[2 * j + h]
            rhs[:, h * 128 : (h + 1) * 128] = block.reshape(1024, 128)
        for ri in range(2):
            for part in range(2):
                start = ri * 512 + part * 256
                got = dot(fwd[start : start + 256, :], rhs[...]).astype(BF16).reshape(16, 16, 256)
                for h in range(2):
                    spec[part * 16 : (part + 1) * 16, 2 * j + h, :, ri * 128 : (ri + 1) * 128] = got[
                        :, :, h * 128 : (h + 1) * 128
                    ]

    @pl.loop(0, 32, unroll=4)
    def _(slot):
        val = spec[slot].reshape(128, 256)
        mixed[slot] = mix_apply(val, mix_matrix(mix, slot), adjoint).reshape(8, 16, 256)
        if accumulate is not None:
            accumulate(slot, val)

    @pl.loop(0, 4)
    def _(j):
        for h in range(2):
            for ri in range(2):
                rhs[ri * 512 : (ri + 1) * 512, h * 128 : (h + 1) * 128] = mixed[
                    :, 2 * j + h, :, ri * 128 : (ri + 1) * 128
                ].reshape(512, 128)
        for part in range(4):
            got = dot(inv[part * 256 : (part + 1) * 256, :], rhs[...]).astype(BF16)
            for h in range(2):
                piece = got[:, h * 128 : (h + 1) * 128].reshape(2, 8, 16, 128)
                if axis == "x":
                    out[part * 2 : (part + 1) * 2, j, h] = piece
                else:
                    out[2 * j + h, part] = piece


def planes_adjoint_kernel(values, fx, ix, fy, iy, mix_x, mix_y, out, spec_x, spec_y, between, mixed, rhs):
    line_pass("x", True, values, fx, ix, mix_x, between, spec_x, mixed, rhs)
    line_pass("y", True, between, fy, iy, mix_y, out, spec_y, mixed, rhs)


def planes_kernel(
    values, fx, ix, fy, iy, mix_x, mix_y, cot_x, cot_y, table, out, terms, between, spec, mixed, rhs, sums
):
    lane = lax.broadcasted_iota(jnp.int32, (64, 128), 1)

    def add_y(slot, val):
        blocks = gradient_blocks(cot_y[slot].reshape(128, 256), val, slot)
        for ri in range(2):
            at = pl.ds(pl.multiple_of((ri * 32 + slot) * 64, 64), 64)
            sums[at, :] = blocks[ri][64:] + pltpu.roll(blocks[ri][:64], 64, 1)

    def add_x(slot, val):
        blocks = gradient_blocks(cot_x[slot].reshape(128, 256), val, slot)
        for ri in range(2):
            at = pl.ds(pl.multiple_of((ri * 32 + slot) * 64, 64), 64)
            got = blocks[ri][:64] + pltpu.roll(blocks[ri][64:], 64, 1)
            sums[at, :] = jnp.where(lane < 64, got, sums[at, :])

    line_pass("y", False, values, fy, iy, mix_y, between, spec, mixed, rhs, add_y)
    line_pass("x", False, between, fx, ix, mix_x, out, spec, mixed, rhs, add_x)
    to_lags(table, sums, terms)


SPEC = (32, 8, 16, 256)


def planes_adjoint(values, fx, ix, fy, iy, mix_x, mix_y):
    spec = jax.ShapeDtypeStruct(SPEC, BF16)
    return pl.pallas_call(
        planes_adjoint_kernel,
        out_shape=(jax.ShapeDtypeStruct(values.shape, BF16), spec, spec),
        in_specs=whole(7),
        out_specs=tuple(whole(3)),
        scratch_shapes=[
            pltpu.VMEM(values.shape, BF16),
            pltpu.VMEM(SPEC, BF16),
            pltpu.VMEM((1024, 256), BF16),
        ],
        compiler_params=params(44),
        cost_estimate=pl.CostEstimate(flops=10 << 30, bytes_accessed=24 << 20, transcendentals=0),
        name="planes_adjoint",
    )(values, fx, ix, fy, iy, mix_x, mix_y)


def planes(values, fx, ix, fy, iy, mix_x, mix_y, cot_x, cot_y, table):
    return pl.pallas_call(
        planes_kernel,
        out_shape=(
            jax.ShapeDtypeStruct(values.shape, BF16),
            jax.ShapeDtypeStruct((4096, 128), F32),
        ),
        in_specs=whole(10),
        out_specs=tuple(whole(2)),
        scratch_shapes=[
            pltpu.VMEM(values.shape, BF16),
            pltpu.VMEM(SPEC, BF16),
            pltpu.VMEM(SPEC, BF16),
            pltpu.VMEM((1024, 256), BF16),
            pltpu.VMEM((4096, 128), F32),
        ],
        compiler_params=params(44),
        cost_estimate=pl.CostEstimate(flops=12 << 30, bytes_accessed=28 << 20, transcendentals=0),
        name="planes",
    )(values, fx, ix, fy, iy, mix_x, mix_y, cot_x, cot_y, table)


def depth_forward(adjoint, values, fwd, spec, rhs):
    @pl.loop(0, 8)
    def _(j):
        for h in range(2):
            lanes = slice(h * 128, (h + 1) * 128)
            if adjoint:
                rhs[:, lanes] = values[:, 2 * j + h].reshape(512, 128)
            else:
                for zp in range(32):
                    rhs[zp * 16 : (zp + 1) * 16, lanes] = values[2 * j + h, :, zp * 128 : (zp + 1) * 128]
        for ri in range(2):
            got = dot(fwd[ri * 256 : (ri + 1) * 256, :], rhs[...]).astype(BF16).reshape(16, 16, 256)
            for h in range(2):
                spec[:, 2 * j + h, :, ri * 128 : (ri + 1) * 128] = got[:, :, h * 128 : (h + 1) * 128]


def depth_backward(adjoint, spec, inv, mix, out, mixed, rhs):
    @pl.loop(0, 16, unroll=4)
    def _(slot):
        val = spec[slot].reshape(256, 256)
        mixed[slot] = mix_apply(val, mix_matrix(mix, slot), adjoint).reshape(16, 16, 256)

    @pl.loop(0, 8)
    def _(j):
        for h in range(2):
            for ri in range(2):
                rhs[ri * 256 : (ri + 1) * 256, h * 128 : (h + 1) * 128] = mixed[
                    :, 2 * j + h, :, ri * 128 : (ri + 1) * 128
                ].reshape(256, 128)
        for part in range(2):
            got = dot(inv[part * 256 : (part + 1) * 256, :], rhs[...]).astype(BF16)
            for h in range(2):
                lanes = slice(h * 128, (h + 1) * 128)
                if adjoint:
                    for zp in range(16):
                        place = (part * 16 + zp) * 128
                        out[2 * j + h, :, place : place + 128] = got[zp * 16 : (zp + 1) * 16, lanes]
                else:
                    out[part * 16 : (part + 1) * 16, 2 * j + h] = got[:, lanes].reshape(16, 16, 128)


DEPTH_SPEC = (16, 16, 16, 256)


def depth_kernel(values, fwd, inv, mix, out, spec, mixed, rhs):
    depth_forward(False, values, fwd, spec, rhs)
    depth_backward(False, spec, inv, mix, out, mixed, rhs)


def depth_sums_kernel(values, fwd, other, table, spec, terms, rhs, sums):
    lane = lax.broadcasted_iota(jnp.int32, (64, 128), 1)

    depth_forward(True, values, fwd, spec, rhs)

    @pl.loop(0, 16, unroll=4)
    def _(slot):
        val = spec[slot].reshape(256, 256)
        blocks = gradient_blocks(val, other[slot].reshape(256, 256), slot)
        for ri in range(2):
            top, bottom = blocks[ri][:64], pltpu.roll(blocks[ri][64:], 64, 1)
            at = pl.multiple_of((ri * 16 + slot) * 64, 64)
            sums[pl.ds(at, 64), :] = jnp.where(lane < 64, top, 0.0) + bottom
            sums[pl.ds(at + 2048, 64), :] = jnp.where(lane < 64, 0.0, top)

    to_lags(table, sums, terms)


def depth_adjoint_kernel(spec, inv, mix, out, mixed, rhs):
    depth_backward(True, spec, inv, mix, out, mixed, rhs)


def depth(values, fwd, inv, mix):
    return pl.pallas_call(
        depth_kernel,
        out_shape=(
            jax.ShapeDtypeStruct((32, 16, 16, 128), BF16),
            jax.ShapeDtypeStruct(DEPTH_SPEC, BF16),
        ),
        in_specs=whole(4),
        out_specs=tuple(whole(2)),
        scratch_shapes=[pltpu.VMEM(DEPTH_SPEC, BF16), pltpu.VMEM((512, 256), BF16)],
        compiler_params=params(24),
        cost_estimate=pl.CostEstimate(flops=4 << 30, bytes_accessed=10 << 20, transcendentals=0),
        name="depth",
    )(values, fwd, inv, mix)


def depth_sums(values, fwd, other, table):
    return pl.pallas_call(
        depth_sums_kernel,
        out_shape=(
            jax.ShapeDtypeStruct(DEPTH_SPEC, BF16),
            jax.ShapeDtypeStruct((2048, 128), F32),
        ),
        in_specs=whole(4),
        out_specs=tuple(whole(2)),
        scratch_shapes=[pltpu.VMEM((512, 256), BF16), pltpu.VMEM((4096, 128), F32)],
        compiler_params=params(58),
        cost_estimate=pl.CostEstimate(flops=4 << 30, bytes_accessed=8 << 20, transcendentals=0),
        name="depth_sums",
    )(values, fwd, other, table)


def depth_adjoint(spec, inv, mix):
    return pl.pallas_call(
        depth_adjoint_kernel,
        out_shape=jax.ShapeDtypeStruct((16, 16, 4096), BF16),
        in_specs=whole(3),
        out_specs=whole(1)[0],
        scratch_shapes=[pltpu.VMEM(DEPTH_SPEC, BF16), pltpu.VMEM((512, 256), BF16)],
        compiler_params=params(24),
        cost_estimate=pl.CostEstimate(flops=2 << 30, bytes_accessed=6 << 20, transcendentals=0),
        name="depth_adjoint",
    )(spec, inv, mix)


def to_pairs_kernel(src, dst, wide, narrow, came, went):
    arrivals = [pltpu.make_async_copy(src.at[k], wide.at[k], came.at[k]) for k in range(4)]
    departures = [pltpu.make_async_copy(narrow.at[k], dst.at[:, k], went.at[k]) for k in range(4)]
    for copy in arrivals:
        copy.start()
    for k in range(4):
        arrivals[k].wait()
        for zp in range(32):
            narrow[k, zp] = wide[k, :, :, zp * 128 : (zp + 1) * 128]
        departures[k].start()
    for copy in departures:
        copy.wait()


def to_pairs(columns):
    return pl.pallas_call(
        to_pairs_kernel,
        out_shape=jax.ShapeDtypeStruct((32, 4, 4, 16, 128), BF16),
        in_specs=[pl.BlockSpec(memory_space=pltpu.HBM)],
        out_specs=pl.BlockSpec(memory_space=pltpu.HBM),
        scratch_shapes=[
            pltpu.VMEM((4, 4, 16, 4096), BF16),
            pltpu.VMEM((4, 32, 4, 16, 128), BF16),
            pltpu.SemaphoreType.DMA((4,)),
            pltpu.SemaphoreType.DMA((4,)),
        ],
        compiler_params=params(60),
        cost_estimate=pl.CostEstimate(flops=0, bytes_accessed=4 << 20, transcendentals=0),
        name="to_pairs",
    )(columns.reshape(4, 4, 16, 4096)).reshape(32, 16, 16, 128)


def last_kernel(src, kept, got, mask, log_rows, dst, taps_dst, wide, lags, went, done):
    departures = [pltpu.make_async_copy(wide.at[k], dst.at[k], went.at[k]) for k in range(4)]
    for k in range(4):
        for zp in range(32):
            wide[k, :, :, zp * 128 : (zp + 1) * 128] = src[zp, k]
        departures[k].start()
    inside = mask[...]
    for row in range(12):
        sums = kept[row] + got[row].astype(F32)
        other = pltpu.roll(sums, 64, 1)
        for half in range(2):
            axis, lag = (half, row) if row < 8 else (2, 2 * (row - 8) + half)
            value = (other if half else sums)[:, :64]
            lags[axis, lag] = inside * value - log_rows[axis, lag]
    taps_copy = pltpu.make_async_copy(lags, taps_dst, done)
    taps_copy.start()
    for copy in departures:
        copy.wait()
    taps_copy.wait()


def last_stage(pairs, kept, got, mask, log_rows):
    hbm = pl.BlockSpec(memory_space=pltpu.HBM)
    return pl.pallas_call(
        last_kernel,
        out_shape=(
            jax.ShapeDtypeStruct((4, 4, 16, 4096), BF16),
            jax.ShapeDtypeStruct((3, 8, 16, 64), F32),
        ),
        in_specs=whole(5),
        out_specs=(hbm, hbm),
        scratch_shapes=[
            pltpu.VMEM((4, 4, 16, 4096), BF16),
            pltpu.VMEM((3, 8, 16, 64), F32),
            pltpu.SemaphoreType.DMA((4,)),
            pltpu.SemaphoreType.DMA,
        ],
        compiler_params=params(8),
        cost_estimate=pl.CostEstimate(flops=0, bytes_accessed=4 << 20, transcendentals=0),
        name="last_stage",
    )(pairs.reshape(32, 4, 4, 16, 128), kept, got, mask, log_rows)


def dft_tables(row_ids, col_ids, length):
    product = row_ids[:, None] * col_ids[None, :] % length
    angle = product.astype(jnp.float32) * (2.0 * math.pi / length)
    return (jnp.cos(angle), jnp.sin(angle))


def log_terms(taps, row_ids, col_ids, length):
    highest = lax.Precision.HIGHEST
    diag_w = jnp.diagonal(taps.astype(jnp.float32), axis1=2, axis2=3)
    cos_full, sin_full = dft_tables(row_ids, row_ids, length)
    real_z = jnp.einsum("kt,atc->akc", cos_full, diag_w, precision=highest)
    imag_z = -jnp.einsum("kt,atc->akc", sin_full, diag_w, precision=highest)
    modulus = real_z * real_z + imag_z * imag_z
    cos_cols, sin_cols = dft_tables(row_ids, col_ids, length)
    summed = jnp.einsum("kt,akc->atc", cos_cols, real_z / modulus, precision=highest) - jnp.einsum(
        "kt,akc->atc", sin_cols, imag_z / modulus, precision=highest
    )
    return summed / math.sqrt(length)


def own_log_terms(taps, count_px):
    all_ids = jnp.arange(N, dtype=jnp.int32)
    slab_t = N // count_px
    t_ids = lax.axis_index("px") * slab_t + jnp.arange(slab_t, dtype=jnp.int32)
    return log_terms(taps, all_ids, t_ids, N)


def finish_taps(summed, log_part, count_py):
    slab_o = C // count_py
    o_ids = lax.axis_index("py") * slab_o + jnp.arange(slab_o, dtype=jnp.int32)
    channel_ids = jnp.arange(C, dtype=jnp.int32)
    diagonal_sel = (channel_ids[None, :] == o_ids[:, None]).astype(jnp.float32)
    keep_mask = (channel_ids[None, :] <= o_ids[:, None]).astype(jnp.float32)
    return keep_mask * (summed - log_part[:, :, None, :] * diagonal_sel)


def halve_parts(values, dim, axis, bit):
    count = lax.axis_size(axis)
    mine = (lax.axis_index(axis) >> bit) & 1
    keep = lax.dynamic_index_in_dim(values, mine, dim, keepdims=False)
    send = lax.dynamic_index_in_dim(values, 1 - mine, dim, keepdims=False).astype(BF16)
    got = lax.ppermute(send, axis, [(i, i ^ (1 << bit)) for i in range(count)])
    return keep, got


def halve(values, dim, axis, bit):
    keep, got = halve_parts(values, dim, axis, bit)
    return keep + got.astype(F32)


def plane_device(field, cotangent, taps):
    axes = ("px", "py")
    count_px = lax.axis_size("px")
    count_py = lax.axis_size("py")
    shape = field.shape
    count = count_px * count_py
    column_shape = (count, 16, 16, 128)
    plane_shape = (count_px, count_py, 2, 8, 16, 128)

    def exchange(values):
        return lax.all_to_all(values, axes, 0, 0, tiled=True)

    cot_planes = exchange(to_pairs(cotangent.reshape(16, 16, 4096))).reshape(plane_shape)

    small = real_dft(N) + real_dft(N // 2)
    fx, ix, fy, iy, fz, iz = tables(*[jnp.asarray(v, BF16) for v in small])
    mix_x, mix_y, mix_z = mixing(taps, jnp.asarray(line_table(), BF16), jnp.asarray(pair_table(), BF16))
    direct, paired = [jnp.asarray(v, F32) for v in tap_tables()]

    first, field_spec = depth(field.reshape(16, 16, 4096), fz, iz, mix_z)
    first_planes = exchange(first).reshape(plane_shape)

    own_rows = lax.axis_index("py") * 16 + jnp.arange(16, dtype=jnp.int32)
    diagonal = (jnp.arange(C, dtype=jnp.int32)[None, :] == own_rows[:, None]).astype(F32)
    log_rows = own_log_terms(taps, count_px)[:, :, None, :] * diagonal
    fx_then, log_rows = lax.optimization_barrier((fx, log_rows))
    back_one, cot_spec, back_spec = planes_adjoint(cot_planes, fx_then, ix, fy, iy, mix_x, mix_y)
    back_columns = exchange(back_one.reshape(column_shape))

    out, terms_xy = planes(first_planes, fx, ix, fy, iy, mix_x, mix_y, cot_spec, back_spec, direct)
    out_columns = exchange(out.reshape(column_shape))

    def split(terms, rows):
        return halve(terms.reshape(2, 2, 2, rows, 2, 2, 16, 128), 5, "py", 0)

    terms_xy = split(terms_xy, 8)
    terms_xy = halve(terms_xy, 4, "py", 1)

    back_hat, terms_z = depth_sums(back_columns, fz, field_spec, paired)

    terms_z = split(terms_z, 4)
    terms_z = halve(terms_z, 4, "py", 1)
    terms_z, back_hat = lax.optimization_barrier((terms_z, back_hat))
    terms = halve(jnp.concatenate([terms_xy, terms_z], 3), 2, "px", 0)
    grad_field = depth_adjoint(back_hat, iz, mix_z)
    terms, grad_field = lax.optimization_barrier((terms, grad_field))
    terms = halve(terms, 1, "px", 1)
    kept, got = halve_parts(terms, 0, "px", 2)
    o_ids = lax.axis_index("py") * 16 + jnp.arange(16, dtype=jnp.int32)
    channel_ids = jnp.arange(C, dtype=jnp.int32)
    inside = (channel_ids[None, :] <= o_ids[:, None]).astype(F32)
    mapped, grad_taps = last_stage(out_columns, kept, got, inside, log_rows)
    return (mapped.reshape(shape), grad_field.reshape(shape), grad_taps)


def along(values, table, position):
    letters = "abcdef"[: values.ndim]
    target = letters[:position] + "k" + letters[position + 1 :]
    return jnp.einsum(
        letters + ",k" + letters[position] + "->" + target,
        values,
        table,
        preferred_element_type=jnp.float32,
    )


def section(values, position, cos_b, sin_b, turn_sign, factor):
    direct = along(values, cos_b, position)
    crossed = along(values, sin_b, position)
    half = values.shape[-1] // 2
    turned = jnp.concatenate([crossed[..., half:], -crossed[..., :half]], -1)
    return ((direct + turn_sign * turned) * factor).astype(jnp.bfloat16)


def z_forward(values, cos_b, sin_b):
    direct = along(values, cos_b, 3)
    crossed = along(values, sin_b, 3)
    return jnp.concatenate([direct, -crossed], -1).astype(jnp.bfloat16)


def z_inverse(values, cos_b, sin_b, factor):
    half = values.shape[-1] // 2
    real_part = along(values[..., :half], cos_b, 3)
    imag_part = along(values[..., half:], sin_b, 3)
    return ((real_part - imag_part) * factor).astype(jnp.bfloat16)


def spectra(taps_axis, cos_b, sin_b):
    real_w = jnp.einsum("kt,toi->koi", cos_b, taps_axis, preferred_element_type=jnp.float32)
    imag_w = -jnp.einsum("kt,toi->koi", sin_b, taps_axis, preferred_element_type=jnp.float32)
    upper = jnp.concatenate([real_w, -imag_w], 2)
    lower = jnp.concatenate([imag_w, real_w], 2)
    return jnp.concatenate([upper, lower], 1).astype(jnp.bfloat16)


def push(values, matrix, position):
    letters = "abcde"
    return jnp.einsum(
        letters + "," + letters[position] + "fe->abcdf",
        values,
        matrix,
        preferred_element_type=jnp.float32,
    ).astype(jnp.bfloat16)


def pull(values, matrix, position):
    letters = "abcde"
    return jnp.einsum(
        letters + "," + letters[position] + "ef->abcdf",
        values,
        matrix,
        preferred_element_type=jnp.float32,
    ).astype(jnp.bfloat16)


def outer(left, right, position):
    letters = "abcde"
    return jnp.einsum(
        "abcde,abcdf->" + letters[position] + "ef", left, right, preferred_element_type=jnp.float32
    )


def tap_terms(spectral, cos_f, sin_f, split_t, split_o):
    width = spectral.shape[1] // 2
    count = spectral.shape[0]
    real_g = spectral[:, :width, :width] + spectral[:, width:, width:]
    imag_g = spectral[:, :width, width:] - spectral[:, width:, :width]
    cos_r = cos_f.reshape(count, split_t, -1)
    sin_r = sin_f.reshape(count, split_t, -1)
    real_r = real_g.reshape(count, split_o, -1, width)
    imag_r = imag_g.reshape(count, split_o, -1, width)
    highest = lax.Precision.HIGHEST
    return jnp.einsum("kpu,kqvi->pquvi", cos_r, real_r, precision=highest) + jnp.einsum(
        "kpu,kqvi->pquvi", sin_r, imag_r, precision=highest
    )


def line_device(field, cotangent, taps):
    batch_rows = field.shape[0]
    local_x = field.shape[1]
    local_y = field.shape[2]
    count_px = lax.axis_size("px")
    count_py = lax.axis_size("py")
    all_ids = jnp.arange(N, dtype=jnp.int32)
    cos_f, sin_f = dft_tables(all_ids, all_ids, N)
    cos_b = cos_f.astype(jnp.bfloat16)
    sin_b = sin_f.astype(jnp.bfloat16)
    stacked = jnp.concatenate([field, cotangent], 0).reshape(2 * batch_rows, local_x, local_y, N, C)
    spectral = z_forward(stacked, cos_b, sin_b)
    spectral = section(
        lax.all_to_all(spectral, "py", split_axis=3, concat_axis=2, tiled=True),
        2,
        cos_b,
        sin_b,
        1.0,
        1.0,
    )
    spectral = section(
        lax.all_to_all(spectral, "px", split_axis=2, concat_axis=1, tiled=True),
        1,
        cos_b,
        sin_b,
        1.0,
        1.0,
    )
    field_hat = spectral[:batch_rows]
    cot_hat = spectral[batch_rows:]
    count_ky = N // count_px
    count_kz = N // count_py
    ky_ids = lax.axis_index("px") * count_ky + jnp.arange(count_ky, dtype=jnp.int32)
    kz_ids = lax.axis_index("py") * count_kz + jnp.arange(count_kz, dtype=jnp.int32)
    cos_y, sin_y = dft_tables(ky_ids, all_ids, N)
    cos_z, sin_z = dft_tables(kz_ids, all_ids, N)
    lower_mask = jnp.tril(jnp.ones((C, C), jnp.float32))
    masked = (taps.astype(jnp.float32) * lower_mask).astype(jnp.bfloat16)
    mix_x = spectra(masked[0], cos_b, sin_b)
    mix_y = spectra(masked[1], cos_y.astype(jnp.bfloat16), sin_y.astype(jnp.bfloat16))
    mix_z = spectra(masked[2], cos_z.astype(jnp.bfloat16), sin_z.astype(jnp.bfloat16))
    first = push(field_hat, mix_z, 3)
    second = push(first, mix_y, 2)
    out_hat = push(second, mix_x, 1)
    back_two = pull(cot_hat, mix_x, 1)
    back_one = pull(back_two, mix_y, 2)
    back_hat = pull(back_one, mix_z, 3)
    grad_x_spec = outer(cot_hat, second, 1)
    grad_y_spec = outer(back_two, first, 2)
    grad_z_spec = outer(back_one, field_hat, 3)
    returned = section(jnp.concatenate([out_hat, back_hat], 0), 1, cos_b, sin_b, -1.0, 1.0 / N)
    returned = section(
        lax.all_to_all(returned, "px", split_axis=1, concat_axis=2, tiled=True),
        2,
        cos_b,
        sin_b,
        -1.0,
        1.0 / N,
    )
    returned = z_inverse(
        lax.all_to_all(returned, "py", split_axis=2, concat_axis=3, tiled=True),
        cos_b,
        sin_b,
        1.0 / N,
    )
    returned = returned.reshape(2 * batch_rows, local_x, local_y, N * C)
    mapped = returned[:batch_rows]
    grad_field = returned[batch_rows:]
    data_scale = 1.0 / (float(N) ** 4 * math.sqrt(N))
    terms = (
        jnp.stack(
            [
                tap_terms(grad_x_spec, cos_f, sin_f, 1, 1),
                tap_terms(grad_y_spec, cos_y, sin_y, 1, 1),
                tap_terms(grad_z_spec, cos_z, sin_z, 1, 1),
            ],
            2,
        )
        * data_scale
    ).reshape(3, N, C, C)
    summed = lax.psum_scatter(
        terms.astype(jnp.bfloat16), "px", scatter_dimension=1, tiled=True
    ).astype(jnp.float32)
    summed = lax.psum_scatter(
        summed.astype(jnp.bfloat16), "py", scatter_dimension=2, tiled=True
    ).astype(jnp.float32)
    grad_taps = finish_taps(summed, own_log_terms(taps, count_px), count_py)
    return (mapped, grad_field, grad_taps)


def solution(mesh):
    count_px, count_py = mesh.shape["px"], mesh.shape["py"]
    fits = N * C == 128 * count_px * count_py and N == 8 * count_px and N == 16 * count_py
    spec = P(None, "px", "py", None)
    return jax.shard_map(
        plane_device if fits else line_device,
        mesh=mesh,
        in_specs=(spec, spec, P()),
        out_specs=(spec, spec, spec),
        check_vma=False,
    )
```
